32 devices in a mesh: rows: 8 (over y, x, core), cols: 4 (over z).
Axes of the slice: x: 2, y: 2, z: 4, core: 2. Of those that a mesh axis runs over, the one named last changes fastest.
Arguments:
- embeddings: bfloat16 [12288, 128], P('rows'), may hold values from -6 to 6
- length_scale: bfloat16 [12288], P('rows'), may hold values from 0.25 to 0.69921875
- start_vectors: float32 [128, 12288], P('cols', 'rows'), may hold values from -6 to 6
- neighbour_ids: int32 [48, 12], P('rows'), may hold values from 0 to 47, as said below
- neighbour_counts: int32 [48], P('rows'), may hold values from 1 to 12
Outputs:
- basis: float32 [128, 12288], P('cols', 'rows')
The draws below stay inside these ranges and needn't reach their ends.
Inputs may be any that keep to these rules, and one draw needn't show every extreme that they name: `neighbour_ids`: slot 0 of a row block names the block itself; the slots from neighbour_counts on repeat the block itself and are unused; the used ids of one block are distinct and name blocks held by the same index of rows or by an index one away along rows.
All inputs are finite; a program needn't handle non-finite values.
Results may differ from the reference program's by a relative error of at most 0.0003.
Values may be sent and summed in bfloat16 or wider, within the bound.
A program may use at most 64 MiB of HBM per device.

```python
import math
import jax
import jax.numpy as jnp
from jax import lax

BS = 256
E = 128
K = 128
MAXNB = 12
ITERS = 3
NB_DEV = 6
NBLK = 48
NPTS = 12288


def neighbour_pattern(key):
    base_key = jax.random.fold_in(key, 4211)
    sub_keys = jax.random.split(base_key, 5)
    devices = NBLK // NB_DEV
    block_ids = jnp.arange(NBLK, dtype=jnp.int32)
    owner_dev = block_ids // NB_DEV
    heavy_dev = jax.random.randint(sub_keys[0], (devices,), 0, 4) == 0
    base_count = jax.random.randint(sub_keys[1], (NBLK,), 1, 5)
    extra_count = jax.random.randint(sub_keys[2], (NBLK,), 0, MAXNB - 3)
    heavy_count = jnp.minimum(base_count + extra_count + 2, MAXNB)
    counts = jnp.where(heavy_dev[owner_dev], heavy_count, base_count)
    counts = jnp.minimum(counts, MAXNB)
    forced_block = jax.random.randint(sub_keys[3], (), 0, NBLK)
    counts = jnp.where(block_ids == forced_block, MAXNB, counts)
    cand_span = 3 * NB_DEV
    cand_off = jnp.arange(cand_span, dtype=jnp.int32)
    candidates = (owner_dev[:, None] - 1) * NB_DEV + cand_off[None, :]
    usable = (candidates >= 0) & (candidates < NBLK) & (candidates != block_ids[:, None])
    scores = jax.random.randint(sub_keys[4], (NBLK, cand_span), 0, 1 << 20)
    rank_key = jnp.where(usable, scores, 1 << 20) * cand_span + cand_off[None, :]
    ordering = jnp.argsort(rank_key, axis=1)
    picked = jnp.take_along_axis(candidates, ordering[:, :MAXNB - 1], axis=1)
    id_table = jnp.concatenate([block_ids[:, None], picked], axis=1)
    slot_pos = jnp.arange(MAXNB, dtype=jnp.int32)
    id_table = jnp.where(slot_pos[None, :] < counts[:, None], id_table, block_ids[:, None])
    return (id_table.astype(jnp.int32), counts.astype(jnp.int32))


def draw_neighbour_ids(key, part):
    id_table, counts = neighbour_pattern(key)
    return id_table


def draw_neighbour_counts(key, part):
    id_table, counts = neighbour_pattern(key)
    return counts


def levels(stream_key, dims, shards, least, high):
    factor_of = 1.0
    for dim, parts in shards:
        steps = jax.random.uniform(jax.random.fold_in(jax.random.fold_in(stream_key, 6), dim), (parts,), jnp.float32, least / len(shards), high / len(shards))
        factor_of = factor_of * jnp.repeat(jnp.exp(steps), dims[dim] // parts).reshape((-1,) + (1,) * (len(dims) - 1 - dim))
    return factor_of


def centred(own_key, extent, spread, reach, cuts=(), held_as=jnp.bfloat16):
    loudness = levels(own_key, extent, cuts, -0.22, 0.18) if cuts else 1.0
    array = jax.random.normal(own_key, extent, jnp.float32) * spread * loudness
    return jnp.minimum(jnp.maximum(array, -reach), reach).astype(held_as)


def setup_inputs(seed: int = 0) -> dict:
    streams_of = jax.random.split(jax.random.key(seed), 6)
    return {
        "embeddings": centred(streams_of[0], (NPTS, E), 1.0, 6.0, ((0, 8),)),
        "length_scale": jnp.clip(jnp.exp(math.log(0.69921875) - 1.0285027 * jax.random.uniform(streams_of[1], (NPTS,), jnp.float32) ** levels(streams_of[1], (NPTS,), ((0, 8),), -0.2, 0.2)), 0.25, 0.69921875).astype(jnp.bfloat16),
        "start_vectors": centred(streams_of[2], (K, NPTS), 1.0, 6.0, ((0, 4), (1, 8)), jnp.float32),
        "neighbour_ids": draw_neighbour_ids(jax.random.fold_in(streams_of[5], 71), 0),
        "neighbour_counts": draw_neighbour_counts(jax.random.fold_in(streams_of[5], 71), 0),
    }


highest = lax.Precision.HIGHEST

def block_tiles(block_id, neighbour_ids, neighbour_counts, blocks_emb, blocks_sq, blocks_bw):
    col_ids = neighbour_ids[block_id]
    row_emb = blocks_emb[block_id].astype(jnp.float32)
    col_emb = blocks_emb[col_ids].astype(jnp.float32)
    inner_prod = jnp.einsum('pe,sqe->spq', row_emb, col_emb)
    distance = blocks_sq[block_id][None, :, None] + blocks_sq[col_ids][:, None, :] - 2.0 * inner_prod
    tile_block = jnp.exp(-distance / (2.0 * E * blocks_bw[block_id][None, :, None] * blocks_bw[col_ids][:, None, :]))
    diagonal_mask = jnp.arange(BS)[:, None] == jnp.arange(BS)[None, :]
    on_self = (col_ids == block_id)[:, None, None] & diagonal_mask[None]
    is_live = (jnp.arange(MAXNB) < neighbour_counts[block_id])[:, None, None]
    tile_block = jnp.where(on_self | jnp.logical_not(is_live), 0.0, tile_block)
    return (tile_block, col_ids)

def reference(embeddings, length_scale, start_vectors, neighbour_ids, neighbour_counts):
    blocks_emb = embeddings.reshape(NBLK, BS, E)
    as_float = embeddings.astype(jnp.float32)
    blocks_sq = lax.optimization_barrier(jnp.sum(as_float * as_float, axis=-1)).reshape(NBLK, BS)
    blocks_bw = length_scale.astype(jnp.float32).reshape(NBLK, BS)
    block_list = jnp.arange(NBLK, dtype=jnp.int32)

    def degree_of(block_id):
        tile_block, col_ids = block_tiles(block_id, neighbour_ids, neighbour_counts, blocks_emb, blocks_sq, blocks_bw)
        return lax.optimization_barrier(jnp.sum(tile_block, axis=(0, 2)))
    degree = lax.map(degree_of, block_list).reshape(NPTS)
    scale = 1.0 / jnp.sqrt(degree)
    iterate = start_vectors
    for iteration in range(ITERS):
        weighted = (iterate * scale[None, :]).reshape(K, NBLK, BS)

        def apply_block(block_id):
            tile_block, col_ids = block_tiles(block_id, neighbour_ids, neighbour_counts, blocks_emb, blocks_sq, blocks_bw)
            return jnp.einsum('ksq,spq->kp', weighted[:, col_ids, :], tile_block, precision=highest)
        product = lax.map(apply_block, block_list).transpose(1, 0, 2).reshape(K, NPTS)
        iterate = 0.5 * (iterate + scale[None, :] * product)
    gram_mat = jnp.dot(iterate, iterate.T, precision=highest) / NPTS
    low_factor = jnp.linalg.cholesky(gram_mat)
    inverse = lax.linalg.triangular_solve(low_factor, jnp.eye(K, dtype=jnp.float32), left_side=True, lower=True)
    return jnp.dot(inverse, iterate, precision=highest)
```

```python
import functools

import jax
import jax.numpy as jnp
from jax import lax
from jax.experimental import pallas as pl
from jax.experimental.pallas import tpu as pltpu
from jax.sharding import PartitionSpec as P

ITERS = 3
ABSENT = float(2 ** 20)
F32 = jnp.float32
BF16 = jnp.bfloat16
highest = lax.Precision.HIGHEST
MESH = pl.DeviceIdType.MESH
VMEM = pl.BlockSpec(memory_space=pltpu.VMEM)
SMEM = pl.BlockSpec(memory_space=pltpu.SMEM)
HBM = pl.BlockSpec(memory_space=pltpu.HBM)
NT = (((1,), (1,)), ((), ()))


def split(value):
    high = value.astype(BF16)
    return high, (value - high.astype(F32)).astype(BF16)


def features(emb, left_side, blocks, extra):
    size, width = emb.shape
    wide = emb.astype(F32)
    norm = jnp.sum(wide * wide, axis=1, keepdims=True)
    part0 = norm.astype(BF16).astype(F32)
    part1 = (norm - part0).astype(BF16).astype(F32)
    part2 = norm - part0 - part1
    lane = lax.broadcasted_iota(jnp.int32, (size, width), 1)
    base = 3 if left_side else 0
    side = jnp.where((lane >= 3 - base) & (lane < 6 - base), 1.0, extra)
    side = jnp.where(lane == base, -part0, side)
    side = jnp.where(lane == base + 1, -part1, side)
    side = jnp.where(lane == base + 2, -part2, side)
    main = wide if left_side else 2.0 * wide
    return jnp.concatenate([main.astype(BF16), side.astype(BF16)], axis=1)


def rate_of(spread, width):
    return (1.4426950408889634 / (2.0 * width)) ** 0.5 / spread


def greet(barrier, peers):
    for peer in peers:
        pl.semaphore_signal(barrier, inc=1, device_id=peer, device_id_type=MESH)
    pl.semaphore_wait(barrier, len(peers))


def spread_out(extent, here, at, sources, lands, send_sem, recv_sem):
    copies = []
    for gap in range(1, extent):
        peer = lax.rem(here + gap, extent)
        copies.append(pltpu.make_async_remote_copy(
            src_ref=sources(peer), dst_ref=lands(here), send_sem=send_sem.at[gap - 1],
            recv_sem=recv_sem.at[gap - 1], device_id=at(peer), device_id_type=MESH))
        copies[-1].start()
    for copy in copies:
        copy.wait()


def steps_kernel(row_extent, col_extent, emb_there, spread, start_there, ids_there,
                 gram_out, turned_out,
                 emb, emb_halo, start, ids, rate, scale, absent, left, left_rate, right,
                 high, low, degree, weighted, change, product, partial, panel, error,
                 pieces, turned, part, part_got, block, block_got, whole, last,
                 own_sem, send_sem, recv_sem, *sems):
    row, col = lax.axis_index("rows"), lax.axis_index("cols")
    blocks, size, width = emb.shape
    slots = ids.shape[1]
    count = start.shape[1]
    band = 3 * blocks

    def along_cols(peer):
        return (row, peer)

    def along_rows(peer):
        return (peer, col)

    barrier = pltpu.get_barrier_semaphore()
    peers = ([along_rows(lax.rem(row + gap, row_extent)) for gap in range(1, row_extent)]
             + [along_cols(lax.rem(col + gap, col_extent)) for gap in range(1, col_extent)])
    for peer in peers:
        pl.semaphore_signal(barrier, inc=1, device_id=peer, device_id_type=MESH)
    own = [pltpu.make_async_copy(source, target, own_sem.at[i]) for i, (source, target) in enumerate(
        [(ids_there, ids), (emb_there, emb), (start_there, start.at[1])])]
    for copy in own:
        copy.start()

    sides = [(row < row_extent - 1, row + 1), (row > 0, row - 1)]

    def copy_of(way, at, source, target, other):
        return pltpu.make_async_remote_copy(
            src_ref=source, dst_ref=target, send_sem=send_sem.at[way, at],
            recv_sem=recv_sem.at[way, at], device_id=(other, col), device_id_type=MESH)

    at_rate, at_start, at_scale, at_emb, at_change = 0, 1, 2, 3, 3 + blocks

    def rate_copy(way, other):
        return copy_of(way, at_rate, rate.at[1], rate.at[2 * way], other)

    def start_copy(way, other):
        return copy_of(way, at_start, start_there, start.at[2 * way], other)

    def scale_copy(way, other):
        return copy_of(way, at_scale, scale.at[1], scale.at[2 * way], other)

    def emb_copy(way, k, other):
        return copy_of(way, at_emb + k, emb_there.at[k], emb_halo.at[way, k], other)

    def change_copy(way, t, k, other):
        return copy_of(way, at_change + blocks * t + k, change.at[t, 1, k],
                       change.at[t, 2 * way, k], other)

    for b in range(blocks):
        rate[1, b] = rate_of(spread[b], width)
    pl.semaphore_wait(barrier, len(peers))
    for way, (there, other) in enumerate(sides):
        @pl.when(there)
        def _():
            rate_copy(way, other).start()
            for k in range(blocks):
                emb_copy(way, k, other).start()

    lane = lax.broadcasted_iota(jnp.int32, (size, width), 1)
    own[0].wait()
    table_row = lax.broadcasted_iota(jnp.int32, absent.shape, 0)
    table_lane = lax.broadcasted_iota(jnp.int32, absent.shape, 1)
    table = jnp.where((table_lane >= 6) & (table_lane < 6 + blocks), -ABSENT, 0.0)
    first = (row - 1) * blocks
    for b in range(blocks):
        for s in range(slots):
            table = jnp.where((table_row == ids[b, s] - first) & (table_lane == 6 + b), 0.0, table)
    absent[...] = table
    own[1].wait()
    for b in range(blocks):
        right[b] = features(emb[b], False, blocks, jnp.where(lane == 6 + b, 1.0, 0.0))
        degree[b] = jnp.zeros(degree.shape[1:], F32)

    def prepare(place, way_emb, c, slot):
        left[slot] = features(way_emb, True, blocks, absent[pl.ds(place * blocks + c, 1), :])
        left_rate[slot] = jnp.broadcast_to(rate[place, c], (128, size)).T

    def tile_of(slot, b):
        gap = lax.dot_general(left[slot], right[b], NT, preferred_element_type=F32)
        factor = jnp.concatenate([left_rate[slot]] * (size // 128), axis=1)
        return jnp.exp2(gap * factor * rate[1, b])

    def keep(b, c, tile):
        top, rest = split(tile)
        high[b, c] = top
        low[b, c] = rest
        degree[b] += jnp.sum(tile.reshape(size // 8, 8, size), axis=0)

    apart = lax.broadcasted_iota(jnp.int32, (size, size), 0) != lax.broadcasted_iota(
        jnp.int32, (size, size), 1
    )

    def own_tiles(c, carry):
        prepare(1, emb[c], c, 0)
        for b in range(blocks):
            keep(b, blocks + c, jnp.where(apart | (c != b), tile_of(0, b), 0.0))
        return carry

    lax.fori_loop(0, blocks, own_tiles, 0)
    own[2].wait()

    for way, (there, other) in enumerate(sides):
        @pl.when(there)
        def _():
            start_copy(way, other).start()

    for way in range(2):
        source_there, source = sides[1 - way]

        @pl.when(source_there)
        def _():
            rate_copy(way, source).wait_recv()

        @pl.when(jnp.logical_not(source_there))
        def _():
            rate[2 * way] = jnp.ones(rate.shape[1:], F32)
            scale[2 * way] = jnp.zeros(scale.shape[1:], F32)
            start[2 * way] = jnp.zeros(start.shape[1:], F32)
            emb_halo[way] = jnp.zeros(emb_halo.shape[1:], BF16)
            for t in range(ITERS - 1):
                change[t, 2 * way] = jnp.zeros(change.shape[2:], BF16)

    def halo_tiles(k, carry):
        for way in range(2):
            source_there, source = sides[1 - way]

            @pl.when(source_there)
            def _():
                emb_copy(way, k, source).wait_recv()
        for way in range(2):
            prepare(2 * way, emb_halo[way, k], k, way)
        for way in range(2):
            for b in range(blocks):
                keep(b, 2 * way * blocks + k, tile_of(way, b))
        return carry

    lax.fori_loop(0, blocks, halo_tiles, 0)
    for b in range(blocks):
        scale[1, b] = 1.0 / jnp.sqrt(jnp.sum(degree[b], axis=0, keepdims=True))
    for way, (there, other) in enumerate(sides):
        @pl.when(there)
        def _():
            scale_copy(way, other).start()

    def weigh(place):
        for c in range(blocks):
            top, rest = split(start[place, :, c * size:(c + 1) * size] * scale[place, c])
            weighted[place, c, :count] = top
            weighted[place, c, count:] = rest

    def first_product(b, places):
        total = jnp.zeros((2 * count, size), F32)
        more = jnp.zeros((count, size), F32)
        for place in places:
            for c in range(blocks):
                both = weighted[place, c]
                total += jnp.dot(both, high[b, place * blocks + c], preferred_element_type=F32)
                more += jnp.dot(both[:count], low[b, place * blocks + c],
                                preferred_element_type=F32)
        return total[:count] + total[count:] + more

    def next_product(t, b, places):
        total = jnp.zeros((count, size), F32)
        for place in places:
            for c in range(blocks):
                both = change[t, place, c]
                total += jnp.dot(both, high[b, place * blocks + c], preferred_element_type=F32)
                total += jnp.dot(both, low[b, place * blocks + c], preferred_element_type=F32)
        return total

    weigh(1)
    for b in range(blocks):
        panel[b] = start[1, :, b * size:(b + 1) * size]

    def send_change(t, b):
        for way, (there, other) in enumerate(sides):
            @pl.when(there)
            def _():
                change_copy(way, t, b, other).start()

    for t in range(ITERS):
        def multiply(b, places):
            return first_product(b, places) if t == 0 else next_product(t - 1, b, places)

        def near(b, carry):
            partial[b] = multiply(b, [1])
            return carry

        lax.fori_loop(0, blocks, near, 0)
        for way in range(2):
            source_there, source = sides[1 - way]

            @pl.when(source_there)
            def _():
                if t == 0:
                    start_copy(way, source).wait_recv()
                    scale_copy(way, source).wait_recv()
                else:
                    for k in range(blocks):
                        change_copy(way, t - 1, k, source).wait_recv()
        if t == 0:
            weigh(0)
            weigh(2)

        def far(b, carry):
            total = partial[b] + multiply(b, [0, 2])
            if t > 0:
                total += 0.5 * product[b]
            factor = scale[1, b]
            panel[b] = 0.5 * (panel[b] + factor * total)
            if t < ITERS - 1:
                product[b] = total
                step = 0.5 * (factor * factor * total)
                if t > 0:
                    step += 0.5 * error[b]
                sent = step.astype(BF16)
                error[b] = step - sent.astype(F32)
                change[t, 1, b] = sent
                send_change(t, b)
            return carry

        lax.fori_loop(0, blocks, far, 0)

    piece = pieces.shape[2]
    points = blocks * size
    columns = count * col_extent
    flat = jnp.concatenate([panel[b] for b in range(blocks)], axis=1)
    for peer in range(col_extent):
        pieces[peer] = flat[:, peer * piece:(peer + 1) * piece]
    spread_out(col_extent, col, along_cols, lambda peer: pieces.at[peer],
               lambda me: turned.at[me], sems[0], sems[1])
    turned[col] = pieces[col]
    vecs = turned[...].reshape(columns, piece)
    turned_out[...] = vecs
    part[...] = lax.dot_general(
        vecs, vecs, NT, precision=highest, preferred_element_type=F32
    ).reshape(part.shape)
    spread_out(col_extent, col, along_cols, lambda peer: part.at[peer],
               lambda me: part_got.at[me], sems[2], sems[3])
    part_got[col] = part[col]
    block[...] = sum(part_got[peer] for peer in range(col_extent))
    spread_out(row_extent, row, along_rows, lambda peer: block,
               lambda me: block_got.at[me], sems[4], sems[5])
    block_got[row] = block[...]
    last[...] = sum(block_got[peer] for peer in range(row_extent)) / (points * row_extent)
    spread_out(col_extent, col, along_cols, lambda peer: last,
               lambda me: whole.at[me], sems[6], sems[7])
    whole[col] = last[...]
    gram_out[...] = whole[...].reshape(columns, columns)

    for way, (there, other) in enumerate(sides):
        @pl.when(there)
        def _():
            rate_copy(way, other).wait_send()
            start_copy(way, other).wait_send()
            scale_copy(way, other).wait_send()
            for k in range(blocks):
                emb_copy(way, k, other).wait_send()
                for t in range(ITERS - 1):
                    change_copy(way, t, k, other).wait_send()


def inverse_factor(matrix):
    side = matrix.shape[0]
    count = side // 8
    shape = (8, side)
    lane = lax.broadcasted_iota(jnp.int32, shape, 1)
    sub = lax.broadcasted_iota(jnp.int32, shape, 0)
    left = [matrix[8 * g:8 * g + 8] for g in range(count)]
    right = [jnp.where(lane == sub + 8 * g, 1.0, 0.0) for g in range(count)]

    def spread_column(value, j):
        return jnp.broadcast_to(value[:, j:j + 1], shape)

    def spread_row(value, i):
        return jnp.broadcast_to(value[i:i + 1], shape)

    out = []
    for g in range(count):
        first = 8 * g
        column = [spread_column(left[g], first + k) for k in range(8)]
        entry = {(i, k): spread_row(column[k], i) for k in range(8) for i in range(k, 8)}
        inv, mult = [], {}
        for k in range(8):
            inv.append(1.0 / entry[k, k])
            for i in range(k + 1, 8):
                mult[i, k] = entry[i, k] * inv[k]
            for l in range(k + 1, 8):
                for i in range(l, 8):
                    entry[i, l] = entry[i, l] - mult[i, k] * entry[l, k]
        rows = []
        for i in range(8):
            a, w = spread_row(left[g], i), spread_row(right[g], i)
            for k in range(i):
                a = a - mult[i, k] * rows[k][0]
                w = w - mult[i, k] * rows[k][1]
            rows.append((a, w))
        done = jnp.zeros(shape, F32)
        for i in range(8):
            done = jnp.where(sub == i, rows[i][1] * (1.0 / jnp.sqrt(entry[i, i])), done)
        out.append(done)
        solved = [None] * 8
        for i in reversed(range(8)):
            a, w = rows[i][0] * inv[i], rows[i][1] * inv[i]
            for k in range(i + 1, 8):
                a = a - mult[k, i] * solved[k][0]
                w = w - mult[k, i] * solved[k][1]
            solved[i] = (a, w)
        for h in range(g + 1, count):
            a, w = left[h], right[h]
            for k in range(8):
                factor = spread_column(left[h], first + k)
                a = a - factor * solved[k][0]
                w = w - factor * solved[k][1]
            left[h], right[h] = a, w
    return jnp.concatenate(out, axis=0)


def basis_kernel(gram, turned, basis):
    inverse = inverse_factor(gram[...])
    basis[...] = jnp.dot(
        inverse, turned[...], precision=highest, preferred_element_type=F32
    ).reshape(basis.shape)


def return_kernel(col_extent, basis, out, land, send_sem, recv_sem):
    row, col = lax.axis_index("rows"), lax.axis_index("cols")
    piece = basis.shape[-1]

    def along_cols(peer):
        return (row, peer)

    greet(pltpu.get_barrier_semaphore(),
          [along_cols(lax.rem(col + gap, col_extent)) for gap in range(1, col_extent)])
    spread_out(col_extent, col, along_cols, lambda peer: basis.at[peer],
               lambda me: land.at[me], send_sem, recv_sem)
    land[col] = basis[col]
    for peer in range(col_extent):
        out[:, peer * piece:(peer + 1) * piece] = land[peer]


def held(value):
    return pltpu.with_memory_space_constraint(value, pltpu.HBM)


def params(**others):
    return pltpu.CompilerParams(vmem_limit_bytes=12 << 20, **others)


def local(row_extent, col_extent, embeddings, length_scale, start_vectors, neighbour_ids,
          neighbour_counts):
    blocks, slots = neighbour_ids.shape
    points, width = embeddings.shape
    size = points // blocks
    count = start_vectors.shape[0]
    shape = jax.ShapeDtypeStruct
    dma = pltpu.SemaphoreType.DMA
    vmem = pltpu.VMEM
    panel = vmem((blocks, count, size), F32)
    columns = count * col_extent
    piece = points // col_extent
    pieces = vmem((col_extent, count, piece), F32)
    part = vmem((col_extent, count, columns), F32)
    gram, turned = pl.pallas_call(
        functools.partial(steps_kernel, row_extent, col_extent),
        out_shape=[shape((columns, columns), F32), shape((columns, piece), F32)],
        in_specs=[HBM, VMEM, HBM, HBM],
        out_specs=[VMEM] * 2,
        scratch_shapes=[
            vmem((blocks, size, width), BF16),
            vmem((2, blocks, size, width), BF16),
            vmem((3, count, points), F32),
            pltpu.SMEM((blocks, slots), jnp.int32),
            vmem((3, blocks, 1, size), F32),
            vmem((3, blocks, 1, size), F32),
            vmem((-(-3 * blocks // 8) * 8, width), F32),
            vmem((2, size, 2 * width), BF16),
            vmem((2, size, 128), F32),
            vmem((blocks, size, 2 * width), BF16),
            vmem((blocks, 3 * blocks, size, size), BF16),
            vmem((blocks, 3 * blocks, size, size), BF16),
            vmem((blocks, 8, size), F32),
            vmem((3, blocks, 2 * count, size), BF16),
            vmem((ITERS - 1, 3, blocks, count, size), BF16),
            panel, panel, panel, panel,
            pieces, pieces, part, part, vmem((count, columns), F32),
            vmem((row_extent, count, columns), F32), part, vmem((count, columns), F32),
            dma((3,)), dma((2, 3 + ITERS * blocks)), dma((2, 3 + ITERS * blocks)),
        ]
        + [dma((extent - 1,)) for extent in (col_extent, col_extent, row_extent, col_extent)
           for _ in range(2)],
        compiler_params=pltpu.CompilerParams(
            vmem_limit_bytes=48 << 20, collective_id=0, has_side_effects=True),
        name="steps",
    )(held(embeddings.reshape(blocks, size, width)),
      length_scale.astype(F32).reshape(blocks, 1, size),
      held(start_vectors), held(neighbour_ids))
    basis = pl.pallas_call(
        basis_kernel,
        out_shape=shape((col_extent, count, piece), F32),
        in_specs=[VMEM] * 2,
        out_specs=VMEM,
        compiler_params=params(),
        name="basis",
    )(gram, turned)
    return pl.pallas_call(
        functools.partial(return_kernel, col_extent),
        out_shape=shape((count, points), F32),
        in_specs=[VMEM],
        out_specs=VMEM,
        scratch_shapes=[pieces, dma((col_extent - 1,)), dma((col_extent - 1,))],
        compiler_params=params(collective_id=1, has_side_effects=True),
        name="basis_return",
    )(basis)


def solution(mesh):
    placed = (P("rows", None), P("rows"), P("cols", "rows"), P("rows", None), P("rows"))
    body = functools.partial(local, mesh.shape["rows"], mesh.shape["cols"])
    return jax.shard_map(
        body, mesh=mesh, in_specs=placed, out_specs=P("cols", "rows"), check_vma=False
    )
```

```python
import functools

import jax
import jax.numpy as jnp
from jax import lax
from jax.experimental import pallas as pl
from jax.experimental.pallas import tpu as pltpu
from jax.sharding import PartitionSpec as P

ITERS = 3
OUTER, OWN, PARTNER = range(3)
UNROLL = 3
ABSENT = float(2 ** 20)
F32 = jnp.float32
BF16 = jnp.bfloat16
highest = lax.Precision.HIGHEST
MESH = pl.DeviceIdType.MESH
VMEM = pl.BlockSpec(memory_space=pltpu.VMEM)
SMEM = pl.BlockSpec(memory_space=pltpu.SMEM)
HBM = pl.BlockSpec(memory_space=pltpu.HBM)
NT = (((1,), (1,)), ((), ()))


def split(value):
    high = value.astype(BF16)
    return high, (value - high.astype(F32)).astype(BF16)


def features(emb, left_side, blocks, extra):
    size, width = emb.shape
    wide = emb.astype(F32)
    norm = jnp.sum(wide * wide, axis=1, keepdims=True)
    part0 = norm.astype(BF16).astype(F32)
    part1 = (norm - part0).astype(BF16).astype(F32)
    part2 = norm - part0 - part1
    lane = lax.broadcasted_iota(jnp.int32, (size, width), 1)
    base = 3 if left_side else 0
    side = jnp.where((lane >= 3 - base) & (lane < 6 - base), 1.0, extra)
    side = jnp.where(lane == base, -part0, side)
    side = jnp.where(lane == base + 1, -part1, side)
    side = jnp.where(lane == base + 2, -part2, side)
    main = wide if left_side else 2.0 * wide
    return jnp.concatenate([main.astype(BF16), side.astype(BF16)], axis=1)


def rate_of(spread, width):
    return (1.4426950408889634 / (2.0 * width)) ** 0.5 / spread


def greet(barrier, peers):
    for peer in peers:
        pl.semaphore_signal(barrier, inc=1, device_id=peer, device_id_type=MESH)
    pl.semaphore_wait(barrier, len(peers))


def spread_out(extent, here, at, sources, lands, send_sem, recv_sem):
    copies = []
    for gap in range(1, extent):
        peer = lax.rem(here + gap, extent)
        copies.append(pltpu.make_async_remote_copy(
            src_ref=sources(peer), dst_ref=lands(here), send_sem=send_sem.at[gap - 1],
            recv_sem=recv_sem.at[gap - 1], device_id=at(peer), device_id_type=MESH))
        copies[-1].start()
    for copy in copies:
        copy.wait()


def inverse_factor(matrix, count_of_rows, use):
    side = matrix.shape[0]
    count = side // 8
    shape = (8, side)
    lane = lax.broadcasted_iota(jnp.int32, shape, 1)
    sub = lax.broadcasted_iota(jnp.int32, shape, 0)
    left = [matrix[8 * g:8 * g + 8] for g in range(count)]
    right = [jnp.where(lane == sub + 8 * g, 1.0, 0.0) for g in range(count)]

    def spread_column(value, j):
        return jnp.broadcast_to(value[:, j:j + 1], shape)

    def spread_row(value, i):
        return jnp.broadcast_to(value[i:i + 1], shape)

    out = []
    for g in range(count):
        first = 8 * g
        column = [spread_column(left[g], first + k) for k in range(8)]
        entry = {(i, k): spread_row(column[k], i) for k in range(8) for i in range(k, 8)}
        inv, mult = [], {}
        for k in range(8):
            inv.append(1.0 / entry[k, k])
            for i in range(k + 1, 8):
                mult[i, k] = entry[i, k] * inv[k]
            for l in range(k + 1, 8):
                for i in range(l, 8):
                    entry[i, l] = entry[i, l] - mult[i, k] * entry[l, k]
        rows = []
        for i in range(8):
            a, w = spread_row(left[g], i), spread_row(right[g], i)
            for k in range(i):
                a = a - mult[i, k] * rows[k][0]
                w = w - mult[i, k] * rows[k][1]
            rows.append((a, w))
        done = jnp.zeros(shape, F32)
        for i in range(8):
            done = jnp.where(sub == i, rows[i][1] * (1.0 / jnp.sqrt(entry[i, i])), done)
        out.append(done)
        if (8 * g + 8) % count_of_rows == 0:
            use(8 * g // count_of_rows, jnp.concatenate(out[-(count_of_rows // 8):], axis=0))
        solved = [None] * 8
        for i in reversed(range(8)):
            a, w = rows[i][0] * inv[i], rows[i][1] * inv[i]
            for k in range(i + 1, 8):
                a = a - mult[k, i] * solved[k][0]
                w = w - mult[k, i] * solved[k][1]
            solved[i] = (a, w)
        for h in range(g + 1, count):
            a, w = left[h], right[h]
            for k in range(8):
                factor = spread_column(left[h], first + k)
                a = a - factor * solved[k][0]
                w = w - factor * solved[k][1]
            left[h], right[h] = a, w


def steps_kernel(row_extent, col_extent, emb_there, spread, start_there, ids_there,
                 out,
                 emb, start, ids, rate, scale, absent, left, left_rate, right,
                 high, low, degree, weighted, change, product, partial, panel, error,
                 vecs, basis, part, part_got, block, block_got, whole, last,
                 own_sem, send_sem, recv_sem, piece_send, piece_recv, return_send,
                 return_recv, *sems):
    row, col = lax.axis_index("rows"), lax.axis_index("cols")
    _, blocks, size, width = emb.shape
    slots = ids.shape[1]
    count = start.shape[1]
    piece = vecs.shape[3]

    def along_cols(peer):
        return (row, peer)

    def along_rows(peer):
        return (peer, col)

    barrier = pltpu.get_barrier_semaphore()
    peers = ([along_rows(lax.rem(row + gap, row_extent)) for gap in range(1, row_extent)]
             + [along_cols(lax.rem(col + gap, col_extent)) for gap in range(1, col_extent)])
    for peer in peers:
        pl.semaphore_signal(barrier, inc=1, device_id=peer, device_id_type=MESH)
    own = [pltpu.make_async_copy(source, target, own_sem.at[i]) for i, (source, target) in enumerate(
        [(ids_there, ids), (emb_there, emb.at[OWN]), (start_there, start.at[OWN])])]
    for copy in own:
        copy.start()

    even = lax.rem(row, 2) == 0
    partner = jnp.where(even, row + 1, row - 1)
    outer = jnp.where(even, row - 1, row + 1)
    outer_there = (outer >= 0) & (outer < row_extent)
    rows_at = {OUTER: outer, OWN: row, PARTNER: partner}

    def copy_of(place, at, source, target):
        return pltpu.make_async_remote_copy(
            src_ref=source, dst_ref=target, send_sem=send_sem.at[place, at],
            recv_sem=recv_sem.at[place, at], device_id=(rows_at[place], col), device_id_type=MESH)

    at_emb, at_change = 3, 3 + blocks

    def rate_copy(place):
        return copy_of(place, 0, rate.at[OWN], rate.at[place])

    def start_copy(place):
        return copy_of(place, 1, start_there, start.at[place])

    def scale_copy(place):
        return copy_of(place, 2, scale.at[OWN], scale.at[place])

    def emb_copy(place, k):
        return copy_of(place, at_emb + k, emb_there.at[k], emb.at[place, k])

    def change_copy(place, t, k):
        return copy_of(place, at_change + blocks * t + k, change.at[t, OWN, k],
                       change.at[t, place, k])

    def with_neighbours(action):
        pl.when(outer_there)(lambda: action(OUTER))
        action(PARTNER)

    for b in range(blocks):
        rate[OWN, b] = rate_of(spread[b], width)
    pl.semaphore_wait(barrier, len(peers))

    def send_points(place):
        rate_copy(place).start()
        for k in range(blocks):
            emb_copy(place, k).start()

    with_neighbours(send_points)

    lane = lax.broadcasted_iota(jnp.int32, (size, width), 1)
    own[0].wait()
    table_row = lax.broadcasted_iota(jnp.int32, absent.shape, 0)
    table_lane = lax.broadcasted_iota(jnp.int32, absent.shape, 1)
    table = jnp.where((table_lane >= 6) & (table_lane < 6 + blocks), -ABSENT, 0.0)
    held_by = jnp.where(table_row < blocks, outer, jnp.where(table_row < 2 * blocks, row, partner))
    held_id = held_by * blocks + lax.rem(table_row, blocks)
    for b in range(blocks):
        for s in range(slots):
            table = jnp.where((held_id == ids[b, s]) & (table_lane == 6 + b), 0.0, table)
    absent[...] = table
    own[1].wait()
    for b in range(blocks):
        right[b] = features(emb[OWN, b], False, blocks, jnp.where(lane == 6 + b, 1.0, 0.0))
        degree[b] = jnp.zeros(degree.shape[1:], F32)

    def prepare(place, c):
        left[...] = features(emb[place, c], True, blocks, absent[pl.ds(place * blocks + c, 1), :])
        left_rate[...] = jnp.broadcast_to(rate[place, c], (128, size)).T

    def tile_of(b):
        gap = lax.dot_general(left[...], right[b], NT, preferred_element_type=F32)
        factor = jnp.concatenate([left_rate[...]] * (size // 128), axis=1)
        return jnp.exp2(gap * factor * rate[OWN, b])

    def keep(b, c, tile):
        top, rest = split(tile)
        high[b, c] = top
        low[b, c] = rest
        degree[b] += jnp.sum(tile.reshape(size // 8, 8, size), axis=0)

    apart = lax.broadcasted_iota(jnp.int32, (size, size), 0) != lax.broadcasted_iota(
        jnp.int32, (size, size), 1
    )

    def own_tiles(c, carry):
        prepare(OWN, c)
        for b in range(blocks):
            keep(b, OWN * blocks + c, jnp.where(apart | (c != b), tile_of(b), 0.0))
        return carry

    lax.fori_loop(0, blocks, own_tiles, 0)
    own[2].wait()
    with_neighbours(lambda place: start_copy(place).start())

    @pl.when(outer_there)
    def _():
        rate_copy(OUTER).wait_recv()

    @pl.when(jnp.logical_not(outer_there))
    def _():
        rate[OUTER] = jnp.ones(rate.shape[1:], F32)
        scale[OUTER] = jnp.zeros(scale.shape[1:], F32)
        start[OUTER] = jnp.zeros(start.shape[1:], F32)
        emb[OUTER] = jnp.zeros(emb.shape[1:], BF16)
        for t in range(ITERS - 1):
            change[t, OUTER] = jnp.zeros(change.shape[2:], BF16)

    rate_copy(PARTNER).wait_recv()

    def partner_tiles(c, carry):
        emb_copy(PARTNER, c).wait_recv()
        prepare(PARTNER, c)
        for b in range(blocks):
            keep(b, PARTNER * blocks + c, tile_of(b))
        return carry

    def outer_tiles(c, carry):
        pl.when(outer_there)(lambda: emb_copy(OUTER, c).wait_recv())
        prepare(OUTER, c)
        for b in range(blocks):
            keep(b, OUTER * blocks + c, tile_of(b))
        return carry

    lax.fori_loop(0, blocks, partner_tiles, 0)
    lax.fori_loop(0, blocks, outer_tiles, 0)
    for b in range(blocks):
        scale[OWN, b] = 1.0 / jnp.sqrt(jnp.sum(degree[b], axis=0, keepdims=True))
    with_neighbours(lambda place: scale_copy(place).start())

    def weigh(place):
        for c in range(blocks):
            top, rest = split(start[place, :, c * size:(c + 1) * size] * scale[place, c])
            weighted[place, c, :count] = top
            weighted[place, c, count:] = rest

    def first_product(b, place):
        total = jnp.zeros((2 * count, size), F32)
        more = jnp.zeros((count, size), F32)
        for c in range(blocks):
            both = weighted[place, c]
            total += jnp.dot(both, high[b, place * blocks + c], preferred_element_type=F32)
            more += jnp.dot(both[:count], low[b, place * blocks + c], preferred_element_type=F32)
        return total[:count] + total[count:] + more

    def next_product(t, b, place):
        total = jnp.zeros((count, size), F32)
        for c in range(blocks):
            both = change[t, place, c]
            total += jnp.dot(both, high[b, place * blocks + c], preferred_element_type=F32)
            total += jnp.dot(both, low[b, place * blocks + c], preferred_element_type=F32)
        return total

    def piece_copy(shard, p, target):
        return pltpu.make_async_remote_copy(
            src_ref=vecs.at[shard, p], dst_ref=vecs.at[shard, p], send_sem=piece_send.at[target],
            recv_sem=piece_recv.at[shard], device_id=(row, target), device_id_type=MESH)

    weigh(OWN)
    for b in range(blocks):
        panel[b] = start[OWN, :, b * size:(b + 1) * size]

    def in_turn(body):
        def several(i, carry):
            for k in range(UNROLL):
                body(i * UNROLL + k, carry)
            return carry

        lax.fori_loop(0, blocks // UNROLL, several, 0)

    for t in range(ITERS):
        def multiply(b, place):
            return first_product(b, place) if t == 0 else next_product(t - 1, b, place)

        def arrive(place):
            if t == 0:
                start_copy(place).wait_recv()
                scale_copy(place).wait_recv()
            else:
                for k in range(blocks):
                    change_copy(place, t - 1, k).wait_recv()

        def from_own(b, carry):
            value = multiply(b, OWN)
            if t > 0:
                value += 0.5 * product[b]
            partial[b] = value
            return carry

        def from_partner(b, carry):
            partial[b] += multiply(b, PARTNER)
            return carry

        def from_outer(b, carry):
            total = partial[b] + multiply(b, OUTER)
            factor = scale[OWN, b]
            vec = 0.5 * (panel[b] + factor * total)
            if t == ITERS - 1:
                return vec
            panel[b] = vec
            product[b] = total
            step = 0.5 * (factor * factor * total)
            if t > 0:
                step += 0.5 * error[b]
            sent = step.astype(BF16)
            error[b] = step - sent.astype(F32)
            change[t, OWN, b] = sent
            with_neighbours(lambda place: change_copy(place, t, b).start())
            return carry

        in_turn(from_own)
        arrive(PARTNER)
        if t == 0:
            weigh(PARTNER)
        in_turn(from_partner)
        pl.when(outer_there)(lambda: arrive(OUTER))
        if t == 0:
            weigh(OUTER)
        if t < ITERS - 1:
            in_turn(from_outer)

    points = blocks * size
    columns = count * col_extent
    for b in range(blocks):
        vec = from_outer(b, 0)
        for p in range(col_extent):
            low_end, high_end = max(p * piece, b * size), min((p + 1) * piece, (b + 1) * size)
            if low_end < high_end:
                vecs[col, p, :, low_end - p * piece:high_end - p * piece] = (
                    vec[:, low_end - b * size:high_end - b * size])
                if high_end == (p + 1) * piece:
                    @pl.when(p != col)
                    def _():
                        piece_copy(col, p, p).start()
    for shard in range(col_extent):
        @pl.when(shard != col)
        def _():
            piece_copy(shard, col, shard).wait_recv()
    here = vecs[:, col].reshape(columns, piece)
    part[...] = lax.dot_general(
        here, here, NT, precision=highest, preferred_element_type=F32
    ).reshape(part.shape)
    spread_out(col_extent, col, along_cols, lambda peer: part.at[peer],
               lambda me: part_got.at[me], sems[0], sems[1])
    part_got[col] = part[col]
    block[...] = sum(part_got[peer] for peer in range(col_extent))
    spread_out(row_extent, row, along_rows, lambda peer: block,
               lambda me: block_got.at[me], sems[2], sems[3])
    block_got[row] = block[...]
    last[...] = sum(block_got[peer] for peer in range(row_extent)) / (points * row_extent)
    spread_out(col_extent, col, along_cols, lambda peer: last,
               lambda me: whole.at[me], sems[4], sems[5])
    whole[col] = last[...]

    def return_copy(source, target):
        return pltpu.make_async_remote_copy(
            src_ref=basis.at[target], dst_ref=out.at[source], send_sem=return_send.at[target],
            recv_sem=return_recv.at[source], device_id=(row, target), device_id_type=MESH)

    def give(shard, rows):
        value = jnp.dot(rows, here, precision=highest, preferred_element_type=F32)

        @pl.when(shard == col)
        def _():
            out[shard] = value

        @pl.when(shard != col)
        def _():
            basis[shard] = value
            return_copy(col, shard).start()

    inverse_factor(whole[...].reshape(columns, columns), count, give)
    for shard in range(col_extent):
        @pl.when(shard != col)
        def _():
            piece_copy(col, shard, shard).wait_send()
            return_copy(col, shard).wait_send()
            return_copy(shard, shard).wait_recv()

    def all_sent(place):
        rate_copy(place).wait_send()
        start_copy(place).wait_send()
        scale_copy(place).wait_send()
        for k in range(blocks):
            emb_copy(place, k).wait_send()
            for t in range(ITERS - 1):
                change_copy(place, t, k).wait_send()

    with_neighbours(all_sent)


def held(value):
    return pltpu.with_memory_space_constraint(value, pltpu.HBM)


def params(**others):
    return pltpu.CompilerParams(vmem_limit_bytes=12 << 20, **others)


def local(row_extent, col_extent, embeddings, length_scale, start_vectors, neighbour_ids,
          neighbour_counts):
    blocks, slots = neighbour_ids.shape
    points, width = embeddings.shape
    size = points // blocks
    count = start_vectors.shape[0]
    shape = jax.ShapeDtypeStruct
    dma = pltpu.SemaphoreType.DMA
    vmem = pltpu.VMEM
    panel = vmem((blocks, count, size), F32)
    columns = count * col_extent
    piece = points // col_extent
    part = vmem((col_extent, count, columns), F32)
    basis = pl.pallas_call(
        functools.partial(steps_kernel, row_extent, col_extent),
        out_shape=shape((col_extent, count, piece), F32),
        in_specs=[HBM, VMEM, HBM, HBM],
        out_specs=VMEM,
        scratch_shapes=[
            vmem((3, blocks, size, width), BF16),
            vmem((3, count, points), F32),
            pltpu.SMEM((blocks, slots), jnp.int32),
            vmem((3, blocks, 1, size), F32),
            vmem((3, blocks, 1, size), F32),
            vmem((-(-3 * blocks // 8) * 8, width), F32),
            vmem((size, 2 * width), BF16),
            vmem((size, 128), F32),
            vmem((blocks, size, 2 * width), BF16),
            vmem((blocks, 3 * blocks, size, size), BF16),
            vmem((blocks, 3 * blocks, size, size), BF16),
            vmem((blocks, 8, size), F32),
            vmem((3, blocks, 2 * count, size), BF16),
            vmem((ITERS - 1, 3, blocks, count, size), BF16),
            panel, panel, panel, panel,
            vmem((col_extent, col_extent, count, piece), F32), vmem((col_extent, count, piece), F32),
            part, part, vmem((count, columns), F32),
            vmem((row_extent, count, columns), F32), part, vmem((count, columns), F32),
            dma((3,)), dma((3, 3 + ITERS * blocks)), dma((3, 3 + ITERS * blocks)),
            dma((col_extent,)), dma((col_extent,)), dma((col_extent,)), dma((col_extent,)),
        ]
        + [dma((extent - 1,)) for extent in (col_extent, row_extent, col_extent)
           for _ in range(2)],
        compiler_params=pltpu.CompilerParams(
            vmem_limit_bytes=48 << 20, collective_id=0, has_side_effects=True),
        name="steps",
    )(held(embeddings.reshape(blocks, size, width)),
      length_scale.astype(F32).reshape(blocks, 1, size),
      held(start_vectors), held(neighbour_ids))
    return basis.transpose(1, 0, 2).reshape(count, points)


def solution(mesh):
    placed = (P("rows", None), P("rows"), P("cols", "rows"), P("rows", None), P("rows"))
    body = functools.partial(local, mesh.shape["rows"], mesh.shape["cols"])
    return jax.shard_map(
        body, mesh=mesh, in_specs=placed, out_specs=P("cols", "rows"), check_vma=False
    )
```

```python
import functools

import jax
import jax.numpy as jnp
from jax import lax
from jax.experimental import pallas as pl
from jax.experimental.pallas import tpu as pltpu
from jax.sharding import PartitionSpec as P

ITERS = 3
OUTER, OWN, PARTNER = range(3)
UNROLL = 3
ABSENT = float(2 ** 20)
F32 = jnp.float32
BF16 = jnp.bfloat16
highest = lax.Precision.HIGHEST
MESH = pl.DeviceIdType.MESH
VMEM = pl.BlockSpec(memory_space=pltpu.VMEM)
SMEM = pl.BlockSpec(memory_space=pltpu.SMEM)
HBM = pl.BlockSpec(memory_space=pltpu.HBM)
NT = (((1,), (1,)), ((), ()))


def split(value):
    high = value.astype(BF16)
    return high, (value - high.astype(F32)).astype(BF16)


def features(emb, left_side, blocks, extra):
    size, width = emb.shape
    wide = emb.astype(F32)
    norm = jnp.sum(wide * wide, axis=1, keepdims=True)
    part0 = norm.astype(BF16).astype(F32)
    part1 = (norm - part0).astype(BF16).astype(F32)
    part2 = norm - part0 - part1
    lane = lax.broadcasted_iota(jnp.int32, (size, width), 1)
    base = 3 if left_side else 0
    side = jnp.where((lane >= 3 - base) & (lane < 6 - base), 1.0, extra)
    side = jnp.where(lane == base, -part0, side)
    side = jnp.where(lane == base + 1, -part1, side)
    side = jnp.where(lane == base + 2, -part2, side)
    main = wide if left_side else 2.0 * wide
    return jnp.concatenate([main.astype(BF16), side.astype(BF16)], axis=1)


def rate_of(spread, width):
    return (1.4426950408889634 / (2.0 * width)) ** 0.5 / spread


def greet(barrier, peers):
    for peer in peers:
        pl.semaphore_signal(barrier, inc=1, device_id=peer, device_id_type=MESH)
    pl.semaphore_wait(barrier, len(peers))


def spread_out(extent, here, at, sources, lands, send_sem, recv_sem):
    copies = []
    for gap in range(1, extent):
        peer = lax.rem(here + gap, extent)
        copies.append(pltpu.make_async_remote_copy(
            src_ref=sources(peer), dst_ref=lands(here), send_sem=send_sem.at[gap - 1],
            recv_sem=recv_sem.at[gap - 1], device_id=at(peer), device_id_type=MESH))
        copies[-1].start()
    for copy in copies:
        copy.wait()


def inverse_factor(matrix, count_of_rows, use):
    side = matrix.shape[0]
    count = side // 8
    shape = (8, side)
    lane = lax.broadcasted_iota(jnp.int32, shape, 1)
    sub = lax.broadcasted_iota(jnp.int32, shape, 0)
    left = [matrix[8 * g:8 * g + 8] for g in range(count)]
    right = [jnp.where(lane == sub + 8 * g, 1.0, 0.0) for g in range(count)]

    def spread_column(value, j):
        return jnp.broadcast_to(value[:, j:j + 1], shape)

    def spread_row(value, i):
        return jnp.broadcast_to(value[i:i + 1], shape)

    out = []
    for g in range(count):
        first = 8 * g
        column = [spread_column(left[g], first + k) for k in range(8)]
        entry = {(i, k): spread_row(column[k], i) for k in range(8) for i in range(k, 8)}
        inv, mult = [], {}
        for k in range(8):
            inv.append(1.0 / entry[k, k])
            for i in range(k + 1, 8):
                mult[i, k] = entry[i, k] * inv[k]
            for l in range(k + 1, 8):
                for i in range(l, 8):
                    entry[i, l] = entry[i, l] - mult[i, k] * entry[l, k]
        rows = []
        for i in range(8):
            a, w = spread_row(left[g], i), spread_row(right[g], i)
            for k in range(i):
                a = a - mult[i, k] * rows[k][0]
                w = w - mult[i, k] * rows[k][1]
            rows.append((a, w))
        done = jnp.zeros(shape, F32)
        for i in range(8):
            done = jnp.where(sub == i, rows[i][1] * (1.0 / jnp.sqrt(entry[i, i])), done)
        out.append(done)
        if (8 * g + 8) % count_of_rows == 0:
            use(8 * g // count_of_rows, jnp.concatenate(out[-(count_of_rows // 8):], axis=0))
        solved = [None] * 8
        for i in reversed(range(8)):
            a, w = rows[i][0] * inv[i], rows[i][1] * inv[i]
            for k in range(i + 1, 8):
                a = a - mult[k, i] * solved[k][0]
                w = w - mult[k, i] * solved[k][1]
            solved[i] = (a, w)
        for h in range(g + 1, count):
            a, w = left[h], right[h]
            for k in range(8):
                factor = spread_column(left[h], first + k)
                a = a - factor * solved[k][0]
                w = w - factor * solved[k][1]
            left[h], right[h] = a, w


def steps_kernel(row_extent, col_extent, emb_there, spread, start_there, ids_there,
                 out,
                 emb, start, ids, rate, scale, absent, left, left_rate, right,
                 high, low, degree, weighted, change, product, partial, panel, error,
                 vecs, basis, part, part_got, block, block_got, whole, last,
                 own_sem, send_sem, recv_sem, piece_send, piece_recv, return_send,
                 return_recv, *sems):
    row, col = lax.axis_index("rows"), lax.axis_index("cols")
    _, blocks, size, width = emb.shape
    slots = ids.shape[1]
    count = start.shape[1]
    piece = vecs.shape[3]

    def along_cols(peer):
        return (row, peer)

    def along_rows(peer):
        return (peer, col)

    barrier = pltpu.get_barrier_semaphore()
    peers = ([along_rows(lax.rem(row + gap, row_extent)) for gap in range(1, row_extent)]
             + [along_cols(lax.rem(col + gap, col_extent)) for gap in range(1, col_extent)])
    for peer in peers:
        pl.semaphore_signal(barrier, inc=1, device_id=peer, device_id_type=MESH)
    own = [pltpu.make_async_copy(source, target, own_sem.at[i]) for i, (source, target) in enumerate(
        [(ids_there, ids), (emb_there, emb.at[OWN]), (start_there, start.at[OWN])])]
    for copy in own:
        copy.start()

    even = lax.rem(row, 2) == 0
    partner = jnp.where(even, row + 1, row - 1)
    outer = jnp.where(even, row - 1, row + 1)
    outer_there = (outer >= 0) & (outer < row_extent)
    rows_at = {OUTER: outer, OWN: row, PARTNER: partner}

    def copy_of(place, at, source, target):
        return pltpu.make_async_remote_copy(
            src_ref=source, dst_ref=target, send_sem=send_sem.at[place, at],
            recv_sem=recv_sem.at[place, at], device_id=(rows_at[place], col), device_id_type=MESH)

    at_emb, at_change = 3, 3 + blocks

    def rate_copy(place):
        return copy_of(place, 0, rate.at[OWN], rate.at[place])

    def start_copy(place):
        return copy_of(place, 1, start_there, start.at[place])

    def scale_copy(place):
        return copy_of(place, 2, scale.at[OWN], scale.at[place])

    def emb_copy(place, k):
        return copy_of(place, at_emb + k, emb_there.at[k], emb.at[place, k])

    def change_copy(place, t, k):
        return copy_of(place, at_change + blocks * t + k, change.at[t, OWN, k],
                       change.at[t, place, k])

    def with_neighbours(action):
        pl.when(outer_there)(lambda: action(OUTER))
        action(PARTNER)

    rates = rate_of(spread[...].astype(F32), width)
    lanes = spread.shape[1]
    for b in range(blocks):
        rate[OWN, b] = jnp.concatenate(
            [rates[k:k + 1] for k in range(b * size // lanes, (b + 1) * size // lanes)], axis=1)
    pl.semaphore_wait(barrier, len(peers))

    def send_points(place):
        rate_copy(place).start()
        for k in range(blocks):
            emb_copy(place, k).start()

    with_neighbours(send_points)

    lane = lax.broadcasted_iota(jnp.int32, (size, width), 1)
    own[0].wait()
    table_row = lax.broadcasted_iota(jnp.int32, absent.shape, 0)
    table_lane = lax.broadcasted_iota(jnp.int32, absent.shape, 1)
    table = jnp.where((table_lane >= 6) & (table_lane < 6 + blocks), -ABSENT, 0.0)
    held_by = jnp.where(table_row < blocks, outer, jnp.where(table_row < 2 * blocks, row, partner))
    held_id = held_by * blocks + lax.rem(table_row, blocks)
    for b in range(blocks):
        for s in range(slots):
            table = jnp.where((held_id == ids[b, s]) & (table_lane == 6 + b), 0.0, table)
    absent[...] = table
    own[1].wait()
    for b in range(blocks):
        right[b] = features(emb[OWN, b], False, blocks, jnp.where(lane == 6 + b, 1.0, 0.0))
        degree[b] = jnp.zeros(degree.shape[1:], F32)

    def prepare(place, c):
        left[...] = features(emb[place, c], True, blocks, absent[pl.ds(place * blocks + c, 1), :])
        left_rate[...] = jnp.broadcast_to(rate[place, c], (128, size)).T

    def tile_of(b):
        gap = lax.dot_general(left[...], right[b], NT, preferred_element_type=F32)
        factor = jnp.concatenate([left_rate[...]] * (size // 128), axis=1)
        return jnp.exp2(gap * factor * rate[OWN, b])

    def keep(b, c, tile):
        top, rest = split(tile)
        high[b, c] = top
        low[b, c] = rest
        degree[b] += jnp.sum(tile.reshape(size // 8, 8, size), axis=0)

    apart = lax.broadcasted_iota(jnp.int32, (size, size), 0) != lax.broadcasted_iota(
        jnp.int32, (size, size), 1
    )

    def own_tiles(c, carry):
        prepare(OWN, c)
        for b in range(blocks):
            keep(b, OWN * blocks + c, jnp.where(apart | (c != b), tile_of(b), 0.0))
        return carry

    lax.fori_loop(0, blocks, own_tiles, 0)
    own[2].wait()
    with_neighbours(lambda place: start_copy(place).start())

    @pl.when(outer_there)
    def _():
        rate_copy(OUTER).wait_recv()

    @pl.when(jnp.logical_not(outer_there))
    def _():
        rate[OUTER] = jnp.ones(rate.shape[1:], F32)
        scale[OUTER] = jnp.zeros(scale.shape[1:], F32)
        start[OUTER] = jnp.zeros(start.shape[1:], F32)
        emb[OUTER] = jnp.zeros(emb.shape[1:], BF16)
        for t in range(ITERS - 1):
            change[t, OUTER] = jnp.zeros(change.shape[2:], BF16)

    rate_copy(PARTNER).wait_recv()

    def partner_tiles(c, carry):
        emb_copy(PARTNER, c).wait_recv()
        prepare(PARTNER, c)
        for b in range(blocks):
            keep(b, PARTNER * blocks + c, tile_of(b))
        return carry

    def outer_tiles(c, carry):
        pl.when(outer_there)(lambda: emb_copy(OUTER, c).wait_recv())
        prepare(OUTER, c)
        for b in range(blocks):
            keep(b, OUTER * blocks + c, tile_of(b))
        return carry

    lax.fori_loop(0, blocks, partner_tiles, 0)
    lax.fori_loop(0, blocks, outer_tiles, 0)
    for b in range(blocks):
        scale[OWN, b] = 1.0 / jnp.sqrt(jnp.sum(degree[b], axis=0, keepdims=True))
    with_neighbours(lambda place: scale_copy(place).start())

    def weigh(place):
        for c in range(blocks):
            top, rest = split(start[place, :, c * size:(c + 1) * size] * scale[place, c])
            weighted[place, c, :count] = top
            weighted[place, c, count:] = rest

    def first_product(b, place):
        total = jnp.zeros((2 * count, size), F32)
        more = jnp.zeros((count, size), F32)
        for c in range(blocks):
            both = weighted[place, c]
            total += jnp.dot(both, high[b, place * blocks + c], preferred_element_type=F32)
            more += jnp.dot(both[:count], low[b, place * blocks + c], preferred_element_type=F32)
        return total[:count] + total[count:] + more

    def next_product(t, b, place, tiles):
        total = jnp.zeros((count, size), F32)
        for c in range(blocks):
            for tile in tiles:
                total += jnp.dot(change[t, place, c], tile[b, place * blocks + c],
                                 preferred_element_type=F32)
        return total

    def piece_copy(shard, p, target):
        return pltpu.make_async_remote_copy(
            src_ref=vecs.at[shard, p], dst_ref=vecs.at[shard, p], send_sem=piece_send.at[target],
            recv_sem=piece_recv.at[shard], device_id=(row, target), device_id_type=MESH)

    weigh(OWN)
    for b in range(blocks):
        panel[b] = start[OWN, :, b * size:(b + 1) * size]

    def in_turn(body, unroll):
        def several(i, carry):
            for k in range(unroll):
                body(i * unroll + k, carry)
            return carry

        lax.fori_loop(0, blocks // unroll, several, 0)

    for t in range(ITERS):
        def multiply(b, place):
            if t == 0:
                return first_product(b, place)
            whole_tiles = place == OWN and t == 1
            return next_product(t - 1, b, place, [high, low] if whole_tiles else [high])

        def arrive(place):
            if t == 0:
                start_copy(place).wait_recv()
                scale_copy(place).wait_recv()
            else:
                for k in range(blocks):
                    change_copy(place, t - 1, k).wait_recv()

        def from_own(b, carry):
            value = multiply(b, OWN)
            if t == 1:
                value += 0.5 * product[b]
            if t > 1:
                late = next_product(t - 2, b, OUTER, [low]) + next_product(t - 2, b, PARTNER, [low])
                panel[b] += 0.5 * (scale[OWN, b] * late)
                value += 0.5 * (product[b] + late)
            partial[b] = value
            return carry

        def from_partner(b, carry):
            partial[b] += multiply(b, PARTNER)
            return carry

        def from_outer(b, carry):
            total = partial[b] + multiply(b, OUTER)
            factor = scale[OWN, b]
            vec = 0.5 * (panel[b] + factor * total)
            if t == ITERS - 1:
                return vec
            panel[b] = vec
            product[b] = total
            step = 0.5 * (factor * factor * total)
            if t > 0:
                step += 0.5 * error[b]
            sent = step.astype(BF16)
            error[b] = step - sent.astype(F32)
            change[t, OWN, b] = sent
            with_neighbours(lambda place: change_copy(place, t, b).start())
            return carry

        in_turn(from_own, blocks)
        arrive(PARTNER)
        if t == 0:
            weigh(PARTNER)
        in_turn(from_partner, blocks)
        pl.when(outer_there)(lambda: arrive(OUTER))
        if t == 0:
            weigh(OUTER)
        if t < ITERS - 1:
            in_turn(from_outer, UNROLL)

    points = blocks * size
    columns = count * col_extent
    for b in range(blocks):
        vec = from_outer(b, 0)
        for p in range(col_extent):
            low_end, high_end = max(p * piece, b * size), min((p + 1) * piece, (b + 1) * size)
            if low_end < high_end:
                vecs[col, p, :, low_end - p * piece:high_end - p * piece] = (
                    vec[:, low_end - b * size:high_end - b * size])
                if high_end == (p + 1) * piece:
                    @pl.when(p != col)
                    def _():
                        piece_copy(col, p, p).start()
    for shard in range(col_extent):
        @pl.when(shard != col)
        def _():
            piece_copy(shard, col, shard).wait_recv()
    here = vecs[:, col].reshape(columns, piece)
    part[...] = lax.dot_general(
        here, here, NT, precision=highest, preferred_element_type=F32
    ).reshape(part.shape)
    spread_out(col_extent, col, along_cols, lambda peer: part.at[peer],
               lambda me: part_got.at[me], sems[0], sems[1])
    part_got[col] = part[col]
    block[...] = sum(part_got[peer] for peer in range(col_extent))
    spread_out(row_extent, row, along_rows, lambda peer: block,
               lambda me: block_got.at[me], sems[2], sems[3])
    block_got[row] = block[...]
    last[...] = sum(block_got[peer] for peer in range(row_extent)) / (points * row_extent)
    spread_out(col_extent, col, along_cols, lambda peer: last,
               lambda me: whole.at[me], sems[4], sems[5])
    whole[col] = last[...]

    def return_copy(source, target):
        return pltpu.make_async_remote_copy(
            src_ref=basis.at[target], dst_ref=out.at[source], send_sem=return_send.at[target],
            recv_sem=return_recv.at[source], device_id=(row, target), device_id_type=MESH)

    def give(shard, rows):
        value = jnp.dot(rows, here, precision=highest, preferred_element_type=F32)

        @pl.when(shard == col)
        def _():
            out[shard] = value

        @pl.when(shard != col)
        def _():
            basis[shard] = value
            return_copy(col, shard).start()

    inverse_factor(whole[...].reshape(columns, columns), count, give)
    for shard in range(col_extent):
        @pl.when(shard != col)
        def _():
            piece_copy(col, shard, shard).wait_send()
            return_copy(col, shard).wait_send()
            return_copy(shard, shard).wait_recv()

    def all_sent(place):
        rate_copy(place).wait_send()
        start_copy(place).wait_send()
        scale_copy(place).wait_send()
        for k in range(blocks):
            emb_copy(place, k).wait_send()
            for t in range(ITERS - 1):
                change_copy(place, t, k).wait_send()

    with_neighbours(all_sent)


def held(value):
    return pltpu.with_memory_space_constraint(value, pltpu.HBM)


def params(**others):
    return pltpu.CompilerParams(vmem_limit_bytes=12 << 20, **others)


def local(row_extent, col_extent, embeddings, length_scale, start_vectors, neighbour_ids,
          neighbour_counts):
    blocks, slots = neighbour_ids.shape
    points, width = embeddings.shape
    size = points // blocks
    count = start_vectors.shape[0]
    shape = jax.ShapeDtypeStruct
    dma = pltpu.SemaphoreType.DMA
    vmem = pltpu.VMEM
    panel = vmem((blocks, count, size), F32)
    columns = count * col_extent
    piece = points // col_extent
    part = vmem((col_extent, count, columns), F32)
    basis = pl.pallas_call(
        functools.partial(steps_kernel, row_extent, col_extent),
        out_shape=shape((col_extent, count, piece), F32),
        in_specs=[HBM, VMEM, HBM, HBM],
        out_specs=VMEM,
        scratch_shapes=[
            vmem((3, blocks, size, width), BF16),
            vmem((3, count, points), F32),
            pltpu.SMEM((blocks, slots), jnp.int32),
            vmem((3, blocks, 1, size), F32),
            vmem((3, blocks, 1, size), F32),
            vmem((-(-3 * blocks // 8) * 8, width), F32),
            vmem((size, 2 * width), BF16),
            vmem((size, 128), F32),
            vmem((blocks, size, 2 * width), BF16),
            vmem((blocks, 3 * blocks, size, size), BF16),
            vmem((blocks, 3 * blocks, size, size), BF16),
            vmem((blocks, 8, size), F32),
            vmem((3, blocks, 2 * count, size), BF16),
            vmem((ITERS - 1, 3, blocks, count, size), BF16),
            panel, panel, panel, panel,
            vmem((col_extent, col_extent, count, piece), F32), vmem((col_extent, count, piece), F32),
            part, part, vmem((count, columns), F32),
            vmem((row_extent, count, columns), F32), part, vmem((count, columns), F32),
            dma((3,)), dma((3, 3 + ITERS * blocks)), dma((3, 3 + ITERS * blocks)),
            dma((col_extent,)), dma((col_extent,)), dma((col_extent,)), dma((col_extent,)),
        ]
        + [dma((extent - 1,)) for extent in (col_extent, row_extent, col_extent)
           for _ in range(2)],
        compiler_params=pltpu.CompilerParams(
            vmem_limit_bytes=48 << 20, collective_id=0, has_side_effects=True),
        name="steps",
    )(held(embeddings.reshape(blocks, size, width)),
      length_scale.reshape(points // 128, 128),
      held(start_vectors), held(neighbour_ids))
    return basis.transpose(1, 0, 2).reshape(count, points)


def solution(mesh):
    placed = (P("rows", None), P("rows"), P("cols", "rows"), P("rows", None), P("rows"))
    body = functools.partial(local, mesh.shape["rows"], mesh.shape["cols"])
    return jax.shard_map(
        body, mesh=mesh, in_specs=placed, out_specs=P("cols", "rows"), check_vma=False
    )
```

```python
import functools

import jax
import jax.numpy as jnp
from jax import lax
from jax.experimental import pallas as pl
from jax.experimental.pallas import tpu as pltpu
from jax.sharding import PartitionSpec as P

ITERS = 3
OUTER, OWN, PARTNER = range(3)
UNROLL = 3
PARTS = 2
ABSENT = float(2 ** 20)
F32 = jnp.float32
BF16 = jnp.bfloat16
highest = lax.Precision.HIGHEST
MESH = pl.DeviceIdType.MESH
VMEM = pl.BlockSpec(memory_space=pltpu.VMEM)
SMEM = pl.BlockSpec(memory_space=pltpu.SMEM)
HBM = pl.BlockSpec(memory_space=pltpu.HBM)
NT = (((1,), (1,)), ((), ()))


def split(value):
    high = value.astype(BF16)
    return high, (value - high.astype(F32)).astype(BF16)


def features(emb, left_side, blocks, extra):
    size, width = emb.shape
    wide = emb.astype(F32)
    norm = jnp.sum(wide * wide, axis=1, keepdims=True)
    part0 = norm.astype(BF16).astype(F32)
    part1 = (norm - part0).astype(BF16).astype(F32)
    part2 = norm - part0 - part1
    lane = lax.broadcasted_iota(jnp.int32, (size, width), 1)
    base = 3 if left_side else 0
    side = jnp.where((lane >= 3 - base) & (lane < 6 - base), 1.0, extra)
    side = jnp.where(lane == base, -part0, side)
    side = jnp.where(lane == base + 1, -part1, side)
    side = jnp.where(lane == base + 2, -part2, side)
    main = wide if left_side else 2.0 * wide
    return jnp.concatenate([main.astype(BF16), side.astype(BF16)], axis=1)


def rate_of(spread, width):
    return (1.4426950408889634 / (2.0 * width)) ** 0.5 / spread


def greet(barrier, peers):
    for peer in peers:
        pl.semaphore_signal(barrier, inc=1, device_id=peer, device_id_type=MESH)
    pl.semaphore_wait(barrier, len(peers))


def spread_out(extent, here, at, sources, lands, send_sem, recv_sem, between=None):
    copies = []
    for gap in range(1, extent):
        peer = lax.rem(here + gap, extent)
        copies.append(pltpu.make_async_remote_copy(
            src_ref=sources(peer), dst_ref=lands(here), send_sem=send_sem.at[gap - 1],
            recv_sem=recv_sem.at[gap - 1], device_id=at(peer), device_id_type=MESH))
        copies[-1].start()
    if between is not None:
        between()
    for copy in copies:
        copy.wait()


def pairs_of(extent):
    load, pairs = {}, []
    for gap in range(extent - 1, 0, -1):
        for i in range(extent - gap):
            ways = []
            for source, target in ((i, i + gap), (i + gap, i)):
                step = 1 if target > source else -1
                links = [(k, k + step) for k in range(source, target, step)]
                ways.append((max(load.get(link, 0) for link in links), source, target, links))
            _, source, target, links = min(ways, key=lambda way: way[0])
            for link in links:
                load[link] = load.get(link, 0) + 1
            pairs.append((source, target))
    return pairs


def inverse_factor(matrix, ends, use):
    side = matrix.shape[0]
    count = side // 8
    shape = (8, side)
    lane = lax.broadcasted_iota(jnp.int32, shape, 1)
    sub = lax.broadcasted_iota(jnp.int32, shape, 0)
    left = [matrix[8 * g:8 * g + 8] for g in range(count)]
    right = [jnp.where(lane == sub + 8 * g, 1.0, 0.0) for g in range(count)]

    def spread_column(value, j):
        return jnp.broadcast_to(value[:, j:j + 1], shape)

    def spread_row(value, i):
        return jnp.broadcast_to(value[i:i + 1], shape)

    panel = min(4, count)
    out, over = [], []
    for g in range(count):
        first = 8 * g
        column = [spread_column(left[g], first + k) for k in range(8)]
        entry = {(i, k): spread_row(column[k], i) for k in range(8) for i in range(k, 8)}
        rows = [(spread_row(left[g], i), spread_row(right[g], i)) for i in range(8)]
        end = (g // panel + 1) * panel
        ahead = g + 1 if g + 1 < end else None
        if ahead is not None:
            factors = [spread_column(left[ahead], first + k) for k in range(8)]
            next_left, next_right = left[ahead], right[ahead]
        mult, pivot, half = {}, {}, {}
        done = [jnp.zeros(shape, F32)] * 2
        for k in range(0, 8, 2):
            a, b, c = entry[k, k], entry[k + 1, k], entry[k + 1, k + 1]
            inv_det = 1.0 / (a * c - b * b)
            ia, ib, ic = c * inv_det, b * inv_det, a * inv_det
            for i in range(k + 2, 8):
                mult[i, k] = entry[i, k] * ia - entry[i, k + 1] * ib
                mult[i, k + 1] = entry[i, k + 1] * ic - entry[i, k] * ib
            for l in range(k + 2, 8):
                for i in range(l, 8):
                    entry[i, l] = entry[i, l] - (
                        mult[i, k] * entry[l, k] + mult[i, k + 1] * entry[l, k + 1])
            (a0, w0), (a1, w1) = rows[k], rows[k + 1]
            half[k] = (ia * a0 - ib * a1, ia * w0 - ib * w1)
            half[k + 1] = (ic * a1 - ib * a0, ic * w1 - ib * w0)
            for i in range(k + 2, 8):
                rows[i] = tuple(
                    value - (mult[i, k] * top + mult[i, k + 1] * low)
                    for value, top, low in zip(rows[i], rows[k], rows[k + 1]))
            if ahead is not None:
                next_left = next_left - (factors[k] * half[k][0] + factors[k + 1] * half[k + 1][0])
                next_right = next_right - (factors[k] * half[k][1] + factors[k + 1] * half[k + 1][1])
                for i in range(k + 2, 8):
                    factors[i] = factors[i] - (
                        mult[i, k] * factors[k] + mult[i, k + 1] * factors[k + 1])
            ratio = b * (1.0 / a)
            own, other = 1.0 / jnp.sqrt(a), 1.0 / jnp.sqrt(c - b * ratio)
            done = [
                jnp.where(sub == k + 1, (low - ratio * top) * other,
                          jnp.where(sub == k, top * own, value))
                for value, top, low in zip(done, rows[k], rows[k + 1])]
        over.append(done[0])
        out.append(done[1])
        solved = [None] * 8
        for k in range(6, -1, -2):
            for j in (k, k + 1):
                solved[j] = tuple(
                    value - sum(mult[i, j] * solved[i][n] for i in range(k + 2, 8))
                    for n, value in enumerate(half[j]))
        for h in range(g + 2, end):
            a, w = left[h], right[h]
            for k in range(8):
                factor = spread_column(left[h], first + k)
                a = a - factor * solved[k][0]
                w = w - factor * solved[k][1]
            left[h], right[h] = a, w
        if ahead is not None:
            left[ahead], right[ahead] = next_left, next_right
        if g + 1 == end and end < count:
            top = jnp.concatenate(over[-panel:], axis=0)
            both = jnp.concatenate([top, jnp.concatenate(out[-panel:], axis=0)], axis=1)
            change = jnp.dot(top.T, both, precision=highest, preferred_element_type=F32)
            for h in range(end, count):
                left[h] = left[h] - change[8 * h:8 * h + 8, :side]
                right[h] = right[h] - change[8 * h:8 * h + 8, side:]
        if 8 * g + 8 in ends:
            begin = max([0] + [end for end in ends if end <= 8 * g])
            use(begin, jnp.concatenate(out[begin // 8:], axis=0))


def steps_kernel(row_extent, col_extent, emb_there, spread, start_there, ids_there,
                 out,
                 emb, start, ids, rate, scale, absent, left, left_rate, right,
                 high, low, degree, weighted, change, product, partial, panel, error,
                 vecs, basis, base, delta, lines, block, block_got, whole, last,
                 own_sem, send_sem, recv_sem, piece_send, piece_recv, return_send,
                 return_recv, base_send, base_recv, delta_send, delta_recv, *sems):
    row, col = lax.axis_index("rows"), lax.axis_index("cols")
    _, blocks, size, width = emb.shape
    slots = ids.shape[1]
    count = start.shape[1]
    piece = vecs.shape[3]

    def along_cols(peer):
        return (row, peer)

    def along_rows(peer):
        return (peer, col)

    barrier = pltpu.get_barrier_semaphore()
    peers = ([along_rows(lax.rem(row + gap, row_extent)) for gap in range(1, row_extent)]
             + [along_cols(lax.rem(col + gap, col_extent)) for gap in range(1, col_extent)])
    for peer in peers:
        pl.semaphore_signal(barrier, inc=1, device_id=peer, device_id_type=MESH)
    own = [pltpu.make_async_copy(source, target, own_sem.at[i]) for i, (source, target) in enumerate(
        [(ids_there, ids), (emb_there, emb.at[OWN]), (start_there, start.at[OWN])])]
    for copy in own:
        copy.start()

    even = lax.rem(row, 2) == 0
    partner = jnp.where(even, row + 1, row - 1)
    outer = jnp.where(even, row - 1, row + 1)
    outer_there = (outer >= 0) & (outer < row_extent)
    rows_at = {OUTER: outer, OWN: row, PARTNER: partner}

    def copy_of(place, at, source, target):
        return pltpu.make_async_remote_copy(
            src_ref=source, dst_ref=target, send_sem=send_sem.at[place, at],
            recv_sem=recv_sem.at[place, at], device_id=(rows_at[place], col), device_id_type=MESH)

    at_emb, at_change = 3, 3 + blocks

    def rate_copy(place):
        return copy_of(place, 0, rate.at[OWN], rate.at[place])

    def start_copy(place):
        return copy_of(place, 1, start_there, start.at[place])

    def scale_copy(place):
        return copy_of(place, 2, scale.at[OWN], scale.at[place])

    def emb_copy(place, k):
        return copy_of(place, at_emb + k, emb_there.at[k], emb.at[place, k])

    def change_copy(place, t, k):
        return copy_of(place, at_change + blocks * t + k, change.at[t, OWN, k],
                       change.at[t, place, k])

    def with_neighbours(action):
        pl.when(outer_there)(lambda: action(OUTER))
        action(PARTNER)

    rates = rate_of(spread[...].astype(F32), width)
    lanes = spread.shape[1]
    for b in range(blocks):
        rate[OWN, b] = jnp.concatenate(
            [rates[k:k + 1] for k in range(b * size // lanes, (b + 1) * size // lanes)], axis=1)
    pl.semaphore_wait(barrier, len(peers))

    def send_points(place):
        rate_copy(place).start()
        for k in range(blocks):
            emb_copy(place, k).start()

    with_neighbours(send_points)

    lane = lax.broadcasted_iota(jnp.int32, (size, width), 1)
    own[0].wait()
    table_row = lax.broadcasted_iota(jnp.int32, absent.shape, 0)
    table_lane = lax.broadcasted_iota(jnp.int32, absent.shape, 1)
    table = jnp.where((table_lane >= 6) & (table_lane < 6 + blocks), -ABSENT, 0.0)
    held_by = jnp.where(table_row < blocks, outer, jnp.where(table_row < 2 * blocks, row, partner))
    held_id = held_by * blocks + lax.rem(table_row, blocks)
    for b in range(blocks):
        for s in range(slots):
            table = jnp.where((held_id == ids[b, s]) & (table_lane == 6 + b), 0.0, table)
    absent[...] = table
    own[1].wait()
    for b in range(blocks):
        right[b] = features(emb[OWN, b], False, blocks, jnp.where(lane == 6 + b, 1.0, 0.0))
        degree[b] = jnp.zeros(degree.shape[1:], F32)

    def prepare(place, c):
        left[...] = features(emb[place, c], True, blocks, absent[pl.ds(place * blocks + c, 1), :])
        left_rate[...] = jnp.broadcast_to(rate[place, c], (128, size)).T

    def tile_of(b):
        gap = lax.dot_general(left[...], right[b], NT, preferred_element_type=F32)
        factor = jnp.concatenate([left_rate[...]] * (size // 128), axis=1)
        return jnp.exp2(gap * factor * rate[OWN, b])

    def keep(b, c, tile):
        top, rest = split(tile)
        high[b, c] = top
        low[b, c] = rest
        degree[b] += jnp.sum(tile.reshape(size // 8, 8, size), axis=0)

    apart = lax.broadcasted_iota(jnp.int32, (size, size), 0) != lax.broadcasted_iota(
        jnp.int32, (size, size), 1
    )

    def own_tiles(c, carry):
        prepare(OWN, c)
        for b in range(blocks):
            keep(b, OWN * blocks + c, jnp.where(apart | (c != b), tile_of(b), 0.0))
        return carry

    lax.fori_loop(0, blocks, own_tiles, 0)
    own[2].wait()
    with_neighbours(lambda place: start_copy(place).start())

    def base_copy(source, target):
        return pltpu.make_async_remote_copy(
            src_ref=start_there, dst_ref=base.at[source], send_sem=base_send.at[target],
            recv_sem=base_recv.at[source], device_id=(row, target), device_id_type=MESH)

    def delta_copy(source, target, b):
        return pltpu.make_async_remote_copy(
            src_ref=delta.at[source, b], dst_ref=delta.at[source, b],
            send_sem=delta_send.at[target, b], recv_sem=delta_recv.at[source, b],
            device_id=(row, target), device_id_type=MESH)

    pairs = pairs_of(col_extent)
    for source, target in pairs:
        @pl.when(col == source)
        def _():
            base_copy(source, target).start()

    lines[...] = jnp.zeros(lines.shape, F32)

    @pl.when(outer_there)
    def _():
        rate_copy(OUTER).wait_recv()

    @pl.when(jnp.logical_not(outer_there))
    def _():
        rate[OUTER] = jnp.ones(rate.shape[1:], F32)
        scale[OUTER] = jnp.zeros(scale.shape[1:], F32)
        start[OUTER] = jnp.zeros(start.shape[1:], F32)
        emb[OUTER] = jnp.zeros(emb.shape[1:], BF16)
        for t in range(ITERS - 1):
            change[t, OUTER] = jnp.zeros(change.shape[2:], BF16)

    rate_copy(PARTNER).wait_recv()

    def partner_tiles(c, carry):
        emb_copy(PARTNER, c).wait_recv()
        prepare(PARTNER, c)
        for b in range(blocks):
            keep(b, PARTNER * blocks + c, tile_of(b))
        return carry

    def outer_tiles(c, carry):
        pl.when(outer_there)(lambda: emb_copy(OUTER, c).wait_recv())
        prepare(OUTER, c)
        for b in range(blocks):
            keep(b, OUTER * blocks + c, tile_of(b))
        return carry

    lax.fori_loop(0, blocks, partner_tiles, 0)
    lax.fori_loop(0, blocks, outer_tiles, 0)
    for b in range(blocks):
        scale[OWN, b] = 1.0 / jnp.sqrt(jnp.sum(degree[b], axis=0, keepdims=True))
    with_neighbours(lambda place: scale_copy(place).start())

    def weigh(place):
        for c in range(blocks):
            top, rest = split(start[place, :, c * size:(c + 1) * size] * scale[place, c])
            weighted[place, c, :count] = top
            weighted[place, c, count:] = rest

    def first_product(b, place):
        total = jnp.zeros((2 * count, size), F32)
        more = jnp.zeros((count, size), F32)
        for c in range(blocks):
            both = weighted[place, c]
            total += jnp.dot(both, high[b, place * blocks + c], preferred_element_type=F32)
            more += jnp.dot(both[:count], low[b, place * blocks + c], preferred_element_type=F32)
        return total[:count] + total[count:] + more

    def next_product(t, b, place, tiles):
        total = jnp.zeros((count, size), F32)
        for c in range(blocks):
            for tile in tiles:
                total += jnp.dot(change[t, place, c], tile[b, place * blocks + c],
                                 preferred_element_type=F32)
        return total

    def piece_copy(shard, p, target):
        return pltpu.make_async_remote_copy(
            src_ref=vecs.at[shard, p], dst_ref=vecs.at[shard, p], send_sem=piece_send.at[target],
            recv_sem=piece_recv.at[shard], device_id=(row, target), device_id_type=MESH)

    weigh(OWN)
    for b in range(blocks):
        panel[b] = start[OWN, :, b * size:(b + 1) * size]

    def in_turn(body, unroll):
        def several(i, carry):
            for k in range(unroll):
                body(i * unroll + k, carry)
            return carry

        lax.fori_loop(0, blocks // unroll, several, 0)

    for t in range(ITERS):
        def multiply(b, place):
            if t == 0:
                return first_product(b, place)
            whole_tiles = place == OWN and t == 1
            return next_product(t - 1, b, place, [high, low] if whole_tiles else [high])

        def arrive(place):
            if t == 0:
                start_copy(place).wait_recv()
                scale_copy(place).wait_recv()
            else:
                for k in range(blocks):
                    change_copy(place, t - 1, k).wait_recv()

        def from_own(b, carry):
            value = multiply(b, OWN)
            if t == 1:
                value += 0.5 * product[b]
            if t > 1:
                late = next_product(t - 2, b, OUTER, [low]) + next_product(t - 2, b, PARTNER, [low])
                panel[b] += 0.5 * (scale[OWN, b] * late)
                value += 0.5 * (product[b] + late)
            partial[b] = value
            return carry

        def from_partner(b, carry):
            partial[b] += multiply(b, PARTNER)
            return carry

        def from_outer(b, carry):
            total = partial[b] + multiply(b, OUTER)
            factor = scale[OWN, b]
            vec = 0.5 * (panel[b] + factor * total)
            if t == ITERS - 1:
                return vec
            panel[b] = vec
            product[b] = total
            step = 0.5 * (factor * factor * total)
            if t > 0:
                step += 0.5 * error[b]
            sent = step.astype(BF16)
            error[b] = step - sent.astype(F32)
            change[t, OWN, b] = sent
            with_neighbours(lambda place: change_copy(place, t, b).start())
            return carry

        in_turn(from_own, blocks)
        arrive(PARTNER)
        if t == 0:
            weigh(PARTNER)
        in_turn(from_partner, blocks)
        pl.when(outer_there)(lambda: arrive(OUTER))
        if t == 0:
            weigh(OUTER)
        if t < ITERS - 1:
            in_turn(from_outer, UNROLL)

    points = blocks * size
    columns = count * col_extent
    for b in range(blocks):
        vec = from_outer(b, 0)
        for p in range(col_extent):
            low_end, high_end = max(p * piece, b * size), min((p + 1) * piece, (b + 1) * size)
            if low_end < high_end:
                vecs[col, p, :, low_end - p * piece:high_end - p * piece] = (
                    vec[:, low_end - b * size:high_end - b * size])
        lines[col, :, b * size:(b + 1) * size] = vec
        delta[col, b] = (vec - 0.5 ** ITERS * start[OWN, :, b * size:(b + 1) * size]).astype(BF16)
        for source, target in pairs:
            @pl.when(col == source)
            def _():
                delta_copy(source, target, b).start()
    for source, target in pairs:
        @pl.when(col == target)
        def _():
            base_copy(source, target).wait_recv()
            for b in range(blocks):
                delta_copy(source, target, b).wait_recv()
                at = slice(b * size, (b + 1) * size)
                lines[source, :, at] = 0.5 ** ITERS * base[source, :, at] + delta[source, b].astype(F32)
    for p in range(col_extent):
        @pl.when(p != col)
        def _():
            piece_copy(col, p, p).start()
    block[...] = lax.dot_general(
        lines[col], lines[...].reshape(columns, points), NT, precision=highest,
        preferred_element_type=F32)

    spread_out(row_extent, row, along_rows, lambda peer: block,
               lambda me: block_got.at[me], sems[0], sems[1])
    block_got[row] = block[...]
    last[...] = sum(block_got[peer] for peer in range(row_extent)) / (points * row_extent)
    spread_out(col_extent, col, along_cols, lambda peer: last,
               lambda me: whole.at[me], sems[2], sems[3])
    whole[col] = last[...]
    half = whole[...].reshape(columns, columns)
    same = lax.broadcasted_iota(jnp.int32, half.shape, 0) // count == lax.broadcasted_iota(
        jnp.int32, half.shape, 1) // count
    gram = jnp.where(same, half, half + half.T)
    for shard in range(col_extent):
        @pl.when(shard != col)
        def _():
            piece_copy(shard, col, shard).wait_recv()
    here = vecs[:, col].reshape(columns, piece)

    fine = max(8, count // PARTS)
    ends = [count * k for k in range(1, col_extent)] + list(
        range(columns - count + fine, columns + 1, fine))
    begins = [0] + ends[:-1]

    def return_copy(source, i):
        target, at = begins[i] // count, begins[i] % count
        span = slice(at, at + ends[i] - begins[i])
        return pltpu.make_async_remote_copy(
            src_ref=basis.at[target, span], dst_ref=out.at[source, span],
            send_sem=return_send.at[i], recv_sem=return_recv.at[source, i],
            device_id=(row, target), device_id_type=MESH)

    def give(begin, rows):
        value = jnp.dot(rows, here, precision=highest, preferred_element_type=F32)
        shard, at = begin // count, begin % count

        @pl.when(shard == col)
        def _():
            out[shard, at:at + rows.shape[0]] = value

        @pl.when(shard != col)
        def _():
            basis[shard, at:at + rows.shape[0]] = value
            return_copy(col, begins.index(begin)).start()

    inverse_factor(gram, ends, give)
    for shard in range(col_extent):
        @pl.when(shard != col)
        def _():
            piece_copy(col, shard, shard).wait_send()
    for i, begin in enumerate(begins):
        shard = begin // count

        @pl.when(shard != col)
        def _():
            return_copy(col, i).wait_send()

        @pl.when(shard == col)
        def _():
            for source in range(col_extent):
                if source != shard:
                    return_copy(source, i).wait_recv()

    for source, target in pairs:
        @pl.when(col == source)
        def _():
            base_copy(source, target).wait_send()
            for b in range(blocks):
                delta_copy(source, target, b).wait_send()

    def all_sent(place):
        rate_copy(place).wait_send()
        start_copy(place).wait_send()
        scale_copy(place).wait_send()
        for k in range(blocks):
            emb_copy(place, k).wait_send()
            for t in range(ITERS - 1):
                change_copy(place, t, k).wait_send()

    with_neighbours(all_sent)


def held(value):
    return pltpu.with_memory_space_constraint(value, pltpu.HBM)


def params(**others):
    return pltpu.CompilerParams(vmem_limit_bytes=12 << 20, **others)


def local(row_extent, col_extent, embeddings, length_scale, start_vectors, neighbour_ids,
          neighbour_counts):
    blocks, slots = neighbour_ids.shape
    points, width = embeddings.shape
    size = points // blocks
    count = start_vectors.shape[0]
    shape = jax.ShapeDtypeStruct
    dma = pltpu.SemaphoreType.DMA
    vmem = pltpu.VMEM
    panel = vmem((blocks, count, size), F32)
    columns = count * col_extent
    piece = points // col_extent
    basis = pl.pallas_call(
        functools.partial(steps_kernel, row_extent, col_extent),
        out_shape=shape((col_extent, count, piece), F32),
        in_specs=[HBM, VMEM, HBM, HBM],
        out_specs=VMEM,
        scratch_shapes=[
            vmem((3, blocks, size, width), BF16),
            vmem((3, count, points), F32),
            pltpu.SMEM((blocks, slots), jnp.int32),
            vmem((3, blocks, 1, size), F32),
            vmem((3, blocks, 1, size), F32),
            vmem((-(-3 * blocks // 8) * 8, width), F32),
            vmem((size, 2 * width), BF16),
            vmem((size, 128), F32),
            vmem((blocks, size, 2 * width), BF16),
            vmem((blocks, 3 * blocks, size, size), BF16),
            vmem((blocks, 3 * blocks, size, size), BF16),
            vmem((blocks, 8, size), F32),
            vmem((3, blocks, 2 * count, size), BF16),
            vmem((ITERS - 1, 3, blocks, count, size), BF16),
            panel, panel, panel, panel,
            vmem((col_extent, col_extent, count, piece), F32), vmem((col_extent, count, piece), F32),
            vmem((col_extent, count, points), F32),
            vmem((col_extent, blocks, count, size), BF16),
            vmem((col_extent, count, points), F32), vmem((count, columns), F32),
            vmem((row_extent, count, columns), F32), vmem((col_extent, count, columns), F32),
            vmem((count, columns), F32),
            dma((3,)), dma((3, 3 + ITERS * blocks)), dma((3, 3 + ITERS * blocks)),
            dma((col_extent,)), dma((col_extent,)),
            dma((col_extent + PARTS - 1,)), dma((col_extent, col_extent + PARTS - 1)),
            dma((col_extent,)), dma((col_extent,)), dma((col_extent, blocks)), dma((col_extent, blocks)),
        ]
        + [dma((extent - 1,)) for extent in (row_extent, col_extent)
           for _ in range(2)],
        compiler_params=pltpu.CompilerParams(
            vmem_limit_bytes=48 << 20, collective_id=0, has_side_effects=True),
        name="steps",
    )(held(embeddings.reshape(blocks, size, width)),
      length_scale.reshape(points // 128, 128),
      held(start_vectors), held(neighbour_ids))
    return basis.transpose(1, 0, 2).reshape(count, points)


def solution(mesh):
    placed = (P("rows", None), P("rows"), P("cols", "rows"), P("rows", None), P("rows"))
    body = functools.partial(local, mesh.shape["rows"], mesh.shape["cols"])
    return jax.shard_map(
        body, mesh=mesh, in_specs=placed, out_specs=P("cols", "rows"), check_vma=False
    )
```

```python
import functools

import jax
import jax.numpy as jnp
from jax import lax
from jax.experimental import pallas as pl
from jax.experimental.pallas import tpu as pltpu
from jax.sharding import PartitionSpec as P

ITERS = 3
OUTER, OWN, PARTNER = range(3)
UNROLL = 6
PARTS = 2
ABSENT = float(2 ** 20)
F32 = jnp.float32
BF16 = jnp.bfloat16
highest = lax.Precision.HIGHEST
MESH = pl.DeviceIdType.MESH
VMEM = pl.BlockSpec(memory_space=pltpu.VMEM)
SMEM = pl.BlockSpec(memory_space=pltpu.SMEM)
HBM = pl.BlockSpec(memory_space=pltpu.HBM)
NT = (((1,), (1,)), ((), ()))


def split(value):
    high = value.astype(BF16)
    return high, (value - high.astype(F32)).astype(BF16)


def features(emb, left_side, blocks, extra):
    size, width = emb.shape
    wide = emb.astype(F32)
    norm = jnp.sum(wide * wide, axis=1, keepdims=True)
    part0 = norm.astype(BF16).astype(F32)
    part1 = (norm - part0).astype(BF16).astype(F32)
    part2 = norm - part0 - part1
    lane = lax.broadcasted_iota(jnp.int32, (size, width), 1)
    base = 3 if left_side else 0
    side = jnp.where((lane >= 3 - base) & (lane < 6 - base), 1.0, extra)
    side = jnp.where(lane == base, -part0, side)
    side = jnp.where(lane == base + 1, -part1, side)
    side = jnp.where(lane == base + 2, -part2, side)
    main = wide if left_side else 2.0 * wide
    return jnp.concatenate([main.astype(BF16), side.astype(BF16)], axis=1)


def rate_of(spread, width):
    return (1.4426950408889634 / (2.0 * width)) ** 0.5 / spread


def greet(barrier, peers):
    for peer in peers:
        pl.semaphore_signal(barrier, inc=1, device_id=peer, device_id_type=MESH)
    pl.semaphore_wait(barrier, len(peers))


def spread_out(extent, here, at, sources, lands, send_sem, recv_sem, between=None):
    copies = []
    for gap in range(1, extent):
        peer = lax.rem(here + gap, extent)
        copies.append(pltpu.make_async_remote_copy(
            src_ref=sources(peer), dst_ref=lands(here), send_sem=send_sem.at[gap - 1],
            recv_sem=recv_sem.at[gap - 1], device_id=at(peer), device_id_type=MESH))
        copies[-1].start()
    if between is not None:
        between()
    for copy in copies:
        copy.wait()


def pairs_of(extent):
    load, pairs = {}, []
    for gap in range(extent - 1, 0, -1):
        for i in range(extent - gap):
            ways = []
            for source, target in ((i, i + gap), (i + gap, i)):
                step = 1 if target > source else -1
                links = [(k, k + step) for k in range(source, target, step)]
                ways.append((max(load.get(link, 0) for link in links), source, target, links))
            _, source, target, links = min(ways, key=lambda way: way[0])
            for link in links:
                load[link] = load.get(link, 0) + 1
            pairs.append((source, target))
    return pairs


def inverse_factor(matrix, ends, use):
    side = matrix.shape[0]
    count = side // 8
    shape = (8, side)
    lane = lax.broadcasted_iota(jnp.int32, shape, 1)
    sub = lax.broadcasted_iota(jnp.int32, shape, 0)
    left = [matrix[8 * g:8 * g + 8] for g in range(count)]
    right = [jnp.where(lane == sub + 8 * g, 1.0, 0.0) for g in range(count)]

    def spread_column(value, j):
        return jnp.broadcast_to(value[:, j:j + 1], shape)

    def spread_row(value, i):
        return jnp.broadcast_to(value[i:i + 1], shape)

    panel = min(4, count)
    out, over = [], []
    for g in range(count):
        first = 8 * g
        column = [spread_column(left[g], first + k) for k in range(8)]
        entry = {(i, k): spread_row(column[k], i) for k in range(8) for i in range(k, 8)}
        rows = [(spread_row(left[g], i), spread_row(right[g], i)) for i in range(8)]
        end = (g // panel + 1) * panel
        ahead = g + 1 if g + 1 < end else None
        if ahead is not None:
            factors = [spread_column(left[ahead], first + k) for k in range(8)]
            next_left, next_right = left[ahead], right[ahead]
        mult, pivot, half = {}, {}, {}
        done = [jnp.zeros(shape, F32)] * 2
        for k in range(0, 8, 2):
            a, b, c = entry[k, k], entry[k + 1, k], entry[k + 1, k + 1]
            inv_det = 1.0 / (a * c - b * b)
            ia, ib, ic = c * inv_det, b * inv_det, a * inv_det
            for i in range(k + 2, 8):
                mult[i, k] = entry[i, k] * ia - entry[i, k + 1] * ib
                mult[i, k + 1] = entry[i, k + 1] * ic - entry[i, k] * ib
            for l in range(k + 2, 8):
                for i in range(l, 8):
                    entry[i, l] = entry[i, l] - (
                        mult[i, k] * entry[l, k] + mult[i, k + 1] * entry[l, k + 1])
            (a0, w0), (a1, w1) = rows[k], rows[k + 1]
            half[k] = (ia * a0 - ib * a1, ia * w0 - ib * w1)
            half[k + 1] = (ic * a1 - ib * a0, ic * w1 - ib * w0)
            for i in range(k + 2, 8):
                rows[i] = tuple(
                    value - (mult[i, k] * top + mult[i, k + 1] * low)
                    for value, top, low in zip(rows[i], rows[k], rows[k + 1]))
            if ahead is not None:
                next_left = next_left - (factors[k] * half[k][0] + factors[k + 1] * half[k + 1][0])
                next_right = next_right - (factors[k] * half[k][1] + factors[k + 1] * half[k + 1][1])
                for i in range(k + 2, 8):
                    factors[i] = factors[i] - (
                        mult[i, k] * factors[k] + mult[i, k + 1] * factors[k + 1])
            ratio = b * (1.0 / a)
            own, other = 1.0 / jnp.sqrt(a), 1.0 / jnp.sqrt(c - b * ratio)
            done = [
                jnp.where(sub == k + 1, (low - ratio * top) * other,
                          jnp.where(sub == k, top * own, value))
                for value, top, low in zip(done, rows[k], rows[k + 1])]
        over.append(done[0])
        out.append(done[1])
        solved = [None] * 8
        for k in range(6, -1, -2):
            for j in (k, k + 1):
                solved[j] = tuple(
                    value - sum(mult[i, j] * solved[i][n] for i in range(k + 2, 8))
                    for n, value in enumerate(half[j]))
        for h in range(g + 2, end):
            a, w = left[h], right[h]
            for k in range(8):
                factor = spread_column(left[h], first + k)
                a = a - factor * solved[k][0]
                w = w - factor * solved[k][1]
            left[h], right[h] = a, w
        if ahead is not None:
            left[ahead], right[ahead] = next_left, next_right
        if g + 1 == end and end < count:
            top = jnp.concatenate(over[-panel:], axis=0)
            both = jnp.concatenate([top, jnp.concatenate(out[-panel:], axis=0)], axis=1)
            change = jnp.dot(top.T, both, precision=highest, preferred_element_type=F32)
            for h in range(end, count):
                left[h] = left[h] - change[8 * h:8 * h + 8, :side]
                right[h] = right[h] - change[8 * h:8 * h + 8, side:]
        if 8 * g + 8 in ends:
            begin = max([0] + [end for end in ends if end <= 8 * g])
            use(begin, jnp.concatenate(out[begin // 8:], axis=0))


def steps_kernel(row_extent, col_extent, emb_there, spread, start_there, ids_there,
                 out,
                 emb, start, ids, rate, scale, absent, left, left_rate, right,
                 high, low, degree, weighted, change, product, partial, panel, error,
                 vecs, basis, base, delta, lines, block, block_got, whole, last,
                 own_sem, send_sem, recv_sem, piece_send, piece_recv, return_send,
                 return_recv, base_send, base_recv, delta_send, delta_recv, *sems):
    row, col = lax.axis_index("rows"), lax.axis_index("cols")
    _, blocks, size, width = emb.shape
    slots = ids.shape[1]
    count = start.shape[1]
    piece = vecs.shape[3]

    def along_cols(peer):
        return (row, peer)

    def along_rows(peer):
        return (peer, col)

    barrier = pltpu.get_barrier_semaphore()
    peers = ([along_rows(lax.rem(row + gap, row_extent)) for gap in range(1, row_extent)]
             + [along_cols(lax.rem(col + gap, col_extent)) for gap in range(1, col_extent)])
    for peer in peers:
        pl.semaphore_signal(barrier, inc=1, device_id=peer, device_id_type=MESH)
    own = [pltpu.make_async_copy(source, target, own_sem.at[i]) for i, (source, target) in enumerate(
        [(ids_there, ids), (emb_there, emb.at[OWN]), (start_there, start.at[OWN])])]
    for copy in own:
        copy.start()

    even = lax.rem(row, 2) == 0
    partner = jnp.where(even, row + 1, row - 1)
    outer = jnp.where(even, row - 1, row + 1)
    outer_there = (outer >= 0) & (outer < row_extent)
    rows_at = {OUTER: outer, OWN: row, PARTNER: partner}

    def copy_of(place, at, source, target):
        return pltpu.make_async_remote_copy(
            src_ref=source, dst_ref=target, send_sem=send_sem.at[place, at],
            recv_sem=recv_sem.at[place, at], device_id=(rows_at[place], col), device_id_type=MESH)

    at_emb, at_change = 3, 3 + blocks

    def rate_copy(place):
        return copy_of(place, 0, rate.at[OWN], rate.at[place])

    def start_copy(place):
        return copy_of(place, 1, start_there, start.at[place])

    def scale_copy(place):
        return copy_of(place, 2, scale.at[OWN], scale.at[place])

    def emb_copy(place, k):
        return copy_of(place, at_emb + k, emb_there.at[k], emb.at[place, k])

    def change_copy(place, t, k):
        return copy_of(place, at_change + blocks * t + k, change.at[t, OWN, k],
                       change.at[t, place, k])

    def with_neighbours(action):
        pl.when(outer_there)(lambda: action(OUTER))
        action(PARTNER)

    rates = rate_of(spread[...].astype(F32), width)
    lanes = spread.shape[1]
    for b in range(blocks):
        rate[OWN, b] = jnp.concatenate(
            [rates[k:k + 1] for k in range(b * size // lanes, (b + 1) * size // lanes)], axis=1)
    lane = lax.broadcasted_iota(jnp.int32, (size, width), 1)
    own[0].wait()
    table_row = lax.broadcasted_iota(jnp.int32, absent.shape, 0)
    table_lane = lax.broadcasted_iota(jnp.int32, absent.shape, 1)
    table = jnp.where((table_lane >= 6) & (table_lane < 6 + blocks), -ABSENT, 0.0)
    held_by = jnp.where(table_row < blocks, outer, jnp.where(table_row < 2 * blocks, row, partner))
    held_id = held_by * blocks + lax.rem(table_row, blocks)
    for b in range(blocks):
        for s in range(slots):
            table = jnp.where((held_id == ids[b, s]) & (table_lane == 6 + b), 0.0, table)
    absent[...] = table
    own[1].wait()
    for b in range(blocks):
        right[b] = features(emb[OWN, b], False, blocks, jnp.where(lane == 6 + b, 1.0, 0.0))
        degree[b] = jnp.zeros(degree.shape[1:], F32)

    def prepare(place, c):
        left[...] = features(emb[place, c], True, blocks, absent[pl.ds(place * blocks + c, 1), :])
        left_rate[...] = jnp.broadcast_to(rate[place, c], (128, size)).T

    def tile_of(b):
        gap = lax.dot_general(left[...], right[b], NT, preferred_element_type=F32)
        factor = jnp.concatenate([left_rate[...]] * (size // 128), axis=1)
        return jnp.exp2(gap * factor * rate[OWN, b])

    def keep(b, c, tile):
        top, rest = split(tile)
        high[b, c] = top
        low[b, c] = rest
        degree[b] += jnp.sum(tile.reshape(size // 8, 8, size), axis=0)

    apart = lax.broadcasted_iota(jnp.int32, (size, size), 0) != lax.broadcasted_iota(
        jnp.int32, (size, size), 1
    )

    def own_tiles(c, carry):
        prepare(OWN, c)
        for b in range(blocks):
            keep(b, OWN * blocks + c, jnp.where(apart | (c != b), tile_of(b), 0.0))
        return carry

    lax.fori_loop(0, 1, own_tiles, 0)
    pl.semaphore_wait(barrier, len(peers))

    def send_points(place):
        rate_copy(place).start()
        for k in range(blocks):
            emb_copy(place, k).start()

    with_neighbours(send_points)

    lax.fori_loop(1, blocks, own_tiles, 0)
    own[2].wait()
    with_neighbours(lambda place: start_copy(place).start())

    def base_copy(source, target):
        return pltpu.make_async_remote_copy(
            src_ref=start_there, dst_ref=base.at[source], send_sem=base_send.at[target],
            recv_sem=base_recv.at[source], device_id=(row, target), device_id_type=MESH)

    def delta_copy(source, target, b):
        return pltpu.make_async_remote_copy(
            src_ref=delta.at[source, b], dst_ref=delta.at[source, b],
            send_sem=delta_send.at[target, b], recv_sem=delta_recv.at[source, b],
            device_id=(row, target), device_id_type=MESH)

    pairs = pairs_of(col_extent)
    for source, target in pairs:
        @pl.when(col == source)
        def _():
            base_copy(source, target).start()

    lines[...] = jnp.zeros(lines.shape, F32)

    @pl.when(outer_there)
    def _():
        rate_copy(OUTER).wait_recv()

    @pl.when(jnp.logical_not(outer_there))
    def _():
        rate[OUTER] = jnp.ones(rate.shape[1:], F32)
        scale[OUTER] = jnp.zeros(scale.shape[1:], F32)
        start[OUTER] = jnp.zeros(start.shape[1:], F32)
        emb[OUTER] = jnp.zeros(emb.shape[1:], BF16)
        for t in range(ITERS - 1):
            change[t, OUTER] = jnp.zeros(change.shape[2:], BF16)

    rate_copy(PARTNER).wait_recv()

    def partner_tiles(c, carry):
        emb_copy(PARTNER, c).wait_recv()
        prepare(PARTNER, c)
        for b in range(blocks):
            keep(b, PARTNER * blocks + c, tile_of(b))
        return carry

    def outer_tiles(c, carry):
        pl.when(outer_there)(lambda: emb_copy(OUTER, c).wait_recv())
        prepare(OUTER, c)
        for b in range(blocks):
            keep(b, OUTER * blocks + c, tile_of(b))
        return carry

    lax.fori_loop(0, blocks, partner_tiles, 0)
    lax.fori_loop(0, blocks, outer_tiles, 0)
    for b in range(blocks):
        scale[OWN, b] = 1.0 / jnp.sqrt(jnp.sum(degree[b], axis=0, keepdims=True))
    with_neighbours(lambda place: scale_copy(place).start())

    def weigh(place):
        for c in range(blocks):
            top, rest = split(start[place, :, c * size:(c + 1) * size] * scale[place, c])
            weighted[place, c, :count] = top
            weighted[place, c, count:] = rest

    def first_product(b, place):
        total = jnp.zeros((2 * count, size), F32)
        more = jnp.zeros((count, size), F32)
        for c in range(blocks):
            both = weighted[place, c]
            total += jnp.dot(both, high[b, place * blocks + c], preferred_element_type=F32)
            more += jnp.dot(both[:count], low[b, place * blocks + c], preferred_element_type=F32)
        return total[:count] + total[count:] + more

    def next_product(t, b, place, tiles):
        total = jnp.zeros((count, size), F32)
        for c in range(blocks):
            for tile in tiles:
                total += jnp.dot(change[t, place, c], tile[b, place * blocks + c],
                                 preferred_element_type=F32)
        return total

    def piece_copy(shard, p, target):
        return pltpu.make_async_remote_copy(
            src_ref=vecs.at[shard, p], dst_ref=vecs.at[shard, p], send_sem=piece_send.at[target],
            recv_sem=piece_recv.at[shard], device_id=(row, target), device_id_type=MESH)

    weigh(OWN)
    for b in range(blocks):
        panel[b] = start[OWN, :, b * size:(b + 1) * size]

    def in_turn(body, unroll):
        def several(i, carry):
            for k in range(unroll):
                body(i * unroll + k, carry)
            return carry

        lax.fori_loop(0, blocks // unroll, several, 0)

    for t in range(ITERS):
        def multiply(b, place):
            if t == 0:
                return first_product(b, place)
            whole_tiles = place == OWN and t == 1
            return next_product(t - 1, b, place, [high, low] if whole_tiles else [high])

        def arrive(place):
            if t == 0:
                start_copy(place).wait_recv()
                scale_copy(place).wait_recv()
            else:
                for k in range(blocks):
                    change_copy(place, t - 1, k).wait_recv()

        def from_own(b, carry):
            value = multiply(b, OWN)
            if t == 1:
                value += 0.5 * product[b]
            if t > 1:
                late = next_product(t - 2, b, OUTER, [low]) + next_product(t - 2, b, PARTNER, [low])
                panel[b] += 0.5 * (scale[OWN, b] * late)
                value += 0.5 * (product[b] + late)
            partial[b] = value
            return carry

        def from_partner(b, carry):
            partial[b] += multiply(b, PARTNER)
            return carry

        def from_outer(b, carry):
            total = partial[b] + multiply(b, OUTER)
            factor = scale[OWN, b]
            vec = 0.5 * (panel[b] + factor * total)
            if t == ITERS - 1:
                return vec
            panel[b] = vec
            product[b] = total
            step = 0.5 * (factor * factor * total)
            if t > 0:
                step += 0.5 * error[b]
            sent = step.astype(BF16)
            error[b] = step - sent.astype(F32)
            change[t, OWN, b] = sent
            with_neighbours(lambda place: change_copy(place, t, b).start())
            return carry

        in_turn(from_own, blocks)
        arrive(PARTNER)
        if t == 0:
            weigh(PARTNER)
        in_turn(from_partner, blocks)
        pl.when(outer_there)(lambda: arrive(OUTER))
        if t == 0:
            weigh(OUTER)
        if t < ITERS - 1:
            in_turn(from_outer, UNROLL)

    points = blocks * size
    columns = count * col_extent
    for b in range(blocks):
        vec = from_outer(b, 0)
        for p in range(col_extent):
            low_end, high_end = max(p * piece, b * size), min((p + 1) * piece, (b + 1) * size)
            if low_end < high_end:
                vecs[col, p, :, low_end - p * piece:high_end - p * piece] = (
                    vec[:, low_end - b * size:high_end - b * size])
        lines[col, :, b * size:(b + 1) * size] = vec
        delta[col, b] = (vec - 0.5 ** ITERS * start[OWN, :, b * size:(b + 1) * size]).astype(BF16)
        for source, target in pairs:
            @pl.when(col == source)
            def _():
                delta_copy(source, target, b).start()
    for source, target in pairs:
        @pl.when(col == target)
        def _():
            base_copy(source, target).wait_recv()
            for b in range(blocks):
                delta_copy(source, target, b).wait_recv()
                at = slice(b * size, (b + 1) * size)
                lines[source, :, at] = 0.5 ** ITERS * base[source, :, at] + delta[source, b].astype(F32)
    for p in range(col_extent):
        @pl.when(p != col)
        def _():
            piece_copy(col, p, p).start()
    block[...] = lax.dot_general(
        lines[col], lines[...].reshape(columns, points), NT, precision=highest,
        preferred_element_type=F32)

    spread_out(row_extent, row, along_rows, lambda peer: block,
               lambda me: block_got.at[me], sems[0], sems[1])
    block_got[row] = block[...]
    last[...] = sum(block_got[peer] for peer in range(row_extent)) / (points * row_extent)
    spread_out(col_extent, col, along_cols, lambda peer: last,
               lambda me: whole.at[me], sems[2], sems[3])
    whole[col] = last[...]
    half = whole[...].reshape(columns, columns)
    same = lax.broadcasted_iota(jnp.int32, half.shape, 0) // count == lax.broadcasted_iota(
        jnp.int32, half.shape, 1) // count
    gram = jnp.where(same, half, half + half.T)
    for shard in range(col_extent):
        @pl.when(shard != col)
        def _():
            piece_copy(shard, col, shard).wait_recv()
    here = vecs[:, col].reshape(columns, piece)

    fine = max(8, count // PARTS)
    ends = [count * k for k in range(1, col_extent)] + list(
        range(columns - count + fine, columns + 1, fine))
    begins = [0] + ends[:-1]

    def return_copy(source, i):
        target, at = begins[i] // count, begins[i] % count
        span = slice(at, at + ends[i] - begins[i])
        return pltpu.make_async_remote_copy(
            src_ref=basis.at[target, span], dst_ref=out.at[source, span],
            send_sem=return_send.at[i], recv_sem=return_recv.at[source, i],
            device_id=(row, target), device_id_type=MESH)

    def give(begin, rows):
        value = jnp.dot(rows, here, precision=highest, preferred_element_type=F32)
        shard, at = begin // count, begin % count

        @pl.when(shard == col)
        def _():
            out[shard, at:at + rows.shape[0]] = value

        @pl.when(shard != col)
        def _():
            basis[shard, at:at + rows.shape[0]] = value
            return_copy(col, begins.index(begin)).start()

    inverse_factor(gram, ends, give)
    for shard in range(col_extent):
        @pl.when(shard != col)
        def _():
            piece_copy(col, shard, shard).wait_send()
    for i, begin in enumerate(begins):
        shard = begin // count

        @pl.when(shard != col)
        def _():
            return_copy(col, i).wait_send()

        @pl.when(shard == col)
        def _():
            for source in range(col_extent):
                if source != shard:
                    return_copy(source, i).wait_recv()

    for source, target in pairs:
        @pl.when(col == source)
        def _():
            base_copy(source, target).wait_send()
            for b in range(blocks):
                delta_copy(source, target, b).wait_send()

    def all_sent(place):
        rate_copy(place).wait_send()
        start_copy(place).wait_send()
        scale_copy(place).wait_send()
        for k in range(blocks):
            emb_copy(place, k).wait_send()
            for t in range(ITERS - 1):
                change_copy(place, t, k).wait_send()

    with_neighbours(all_sent)


def held(value):
    return pltpu.with_memory_space_constraint(value, pltpu.HBM)


def params(**others):
    return pltpu.CompilerParams(vmem_limit_bytes=12 << 20, **others)


def local(row_extent, col_extent, embeddings, length_scale, start_vectors, neighbour_ids,
          neighbour_counts):
    blocks, slots = neighbour_ids.shape
    points, width = embeddings.shape
    size = points // blocks
    count = start_vectors.shape[0]
    shape = jax.ShapeDtypeStruct
    dma = pltpu.SemaphoreType.DMA
    vmem = pltpu.VMEM
    panel = vmem((blocks, count, size), F32)
    columns = count * col_extent
    piece = points // col_extent
    basis = pl.pallas_call(
        functools.partial(steps_kernel, row_extent, col_extent),
        out_shape=shape((col_extent, count, piece), F32),
        in_specs=[HBM, VMEM, HBM, HBM],
        out_specs=VMEM,
        scratch_shapes=[
            vmem((3, blocks, size, width), BF16),
            vmem((3, count, points), F32),
            pltpu.SMEM((blocks, slots), jnp.int32),
            vmem((3, blocks, 1, size), F32),
            vmem((3, blocks, 1, size), F32),
            vmem((-(-3 * blocks // 8) * 8, width), F32),
            vmem((size, 2 * width), BF16),
            vmem((size, 128), F32),
            vmem((blocks, size, 2 * width), BF16),
            vmem((blocks, 3 * blocks, size, size), BF16),
            vmem((blocks, 3 * blocks, size, size), BF16),
            vmem((blocks, 8, size), F32),
            vmem((3, blocks, 2 * count, size), BF16),
            vmem((ITERS - 1, 3, blocks, count, size), BF16),
            panel, panel, panel, panel,
            vmem((col_extent, col_extent, count, piece), F32), vmem((col_extent, count, piece), F32),
            vmem((col_extent, count, points), F32),
            vmem((col_extent, blocks, count, size), BF16),
            vmem((col_extent, count, points), F32), vmem((count, columns), F32),
            vmem((row_extent, count, columns), F32), vmem((col_extent, count, columns), F32),
            vmem((count, columns), F32),
            dma((3,)), dma((3, 3 + ITERS * blocks)), dma((3, 3 + ITERS * blocks)),
            dma((col_extent,)), dma((col_extent,)),
            dma((col_extent + PARTS - 1,)), dma((col_extent, col_extent + PARTS - 1)),
            dma((col_extent,)), dma((col_extent,)), dma((col_extent, blocks)), dma((col_extent, blocks)),
        ]
        + [dma((extent - 1,)) for extent in (row_extent, col_extent)
           for _ in range(2)],
        compiler_params=pltpu.CompilerParams(
            vmem_limit_bytes=48 << 20, collective_id=0, has_side_effects=True),
        name="steps",
    )(held(embeddings.reshape(blocks, size, width)),
      length_scale.reshape(points // 128, 128),
      held(start_vectors), held(neighbour_ids))
    return basis.transpose(1, 0, 2).reshape(count, points)


def solution(mesh):
    placed = (P("rows", None), P("rows"), P("cols", "rows"), P("rows", None), P("rows"))
    body = functools.partial(local, mesh.shape["rows"], mesh.shape["cols"])
    return jax.shard_map(
        body, mesh=mesh, in_specs=placed, out_specs=P("cols", "rows"), check_vma=False
    )
```
